256 devices in a mesh: row: 8 (over y, core), col: 8 (over z), track: 4 (over x).
Axes of the slice: x: 4, y: 4, z: 8, core: 2. Of those that a mesh axis runs over, the one named last changes fastest.
Arguments:
- factors: float32 [16384, 2, 16, 576], P(('row', 'col', 'track')), may hold values from -0.5 to 0.5
- track_clusters: int32 [16384, 2], P(('row', 'col', 'track')), may hold values from 0 to 7, as said below
- filed_flip: int32 [16384], P(('row', 'col', 'track')), may hold values from 0 to 1, as said below
- damping: float32 [8, 576], P('row'), may hold values from 50 to 500
- rhs: float32 [8, 576], P('row'), may hold values from -3000 to 3000
Outputs:
- solution: float32 [8, 576], P('row')
- scaled_residual: float32 [8, 576], P('row')
- filed_blocks: float32 [8, 8, 576, 576], P('row', 'col', 'track')
The draws below stay inside these ranges and needn't reach their ends.
Inputs may be any that keep to these rules, and one draw needn't show every extreme that they name: `track_clusters`: each row names two different clusters, the first below the second. `filed_flip`: the owner of a block filed under (i, j) is the device of row group i // 1 and column j, with the track index of the device that holds the track block. Of the 64 track blocks of one device at most 3 go to any one owner, and in every draw, for each track index, some owner receives exactly 3 from every device of that track index.
All inputs are finite; a program needn't handle non-finite values.
Results may differ from the reference program's by a relative error of at most 0.0003.
Values sent between devices are 32-bit elements; how exact they have to be, the bound alone decides.
No kernel may reach another device: no remote copies, remote signals or barrier semaphores. Data moves between devices by JAX's collectives and lax.ppermute only.
A program may use at most 128 MiB of HBM per device.

```python
import math
import jax
import jax.numpy as jnp
import numpy as np
from jax import lax

CAM_PARAMS = 576
JAC_ROWS = 16
TRACK_BLOCKS_DEV = 64
ITERS = 2
CLUSTERS = 8
ROW_CLUSTERS = 1
CAPACITY = 3
TRACK_BLOCKS = 16384
N_ROW = 8
N_COL = 8
N_TRACK = 4


def filing_plan(key):
    owners = N_ROW * N_COL
    sources = owners * N_TRACK
    owner_table = np.array([candidate for candidate in range(owners) if ROW_CLUSTERS > 1 or candidate // N_COL != candidate % N_COL], dtype=np.int32)
    valid_count = int(owner_table.shape[0])
    base = jax.random.fold_in(key, 7)
    subkeys = jax.random.split(base, 4)
    busiest = jax.random.randint(subkeys[0], (N_TRACK,), 0, valid_count)
    source_track = jnp.arange(sources) % N_TRACK
    busiest_of = busiest[source_track]
    tickets = valid_count * CAPACITY
    ticket_ids = jnp.arange(tickets, dtype=jnp.int32)
    ticket_owner = ticket_ids // CAPACITY
    random_part = jax.random.randint(subkeys[1], (sources, tickets), 0, 1 << 16)
    scores = random_part * tickets + ticket_ids[None, :]
    scores = jnp.where(ticket_owner[None, :] == busiest_of[:, None], -1 - ticket_ids[None, :], scores)
    unused, chosen = lax.top_k(scores, TRACK_BLOCKS_DEV - CAPACITY)
    picked = ticket_owner[chosen]
    targets = jnp.concatenate([jnp.broadcast_to(busiest_of[:, None], (sources, CAPACITY)), picked], axis=1)
    shuffle_keys = jax.random.randint(subkeys[2], (sources, TRACK_BLOCKS_DEV), 0, 1 << 16) * TRACK_BLOCKS_DEV + jnp.arange(TRACK_BLOCKS_DEV)[None, :]
    shuffle = jnp.argsort(shuffle_keys, axis=1, stable=True)
    targets = jnp.take_along_axis(targets, shuffle, axis=1)
    owner = jnp.asarray(owner_table)[targets]
    owner_row = owner // N_COL
    owner_col = owner % N_COL
    offset = jax.random.randint(subkeys[3], owner.shape, 0, ROW_CLUSTERS)
    filed_row = owner_row * ROW_CLUSTERS + offset
    filed_row = jnp.where(filed_row == owner_col, owner_row * ROW_CLUSTERS + (offset + 1) % ROW_CLUSTERS, filed_row)
    low_cluster = jnp.minimum(filed_row, owner_col)
    high_cluster = jnp.maximum(filed_row, owner_col)
    flags = (filed_row > owner_col).astype(jnp.int32)
    pairs = jnp.stack([low_cluster, high_cluster], axis=-1).reshape(TRACK_BLOCKS, 2).astype(jnp.int32)
    return (pairs, flags.reshape(TRACK_BLOCKS))


def draw_track_clusters(key, part):
    return filing_plan(key)[0]


def draw_filed_flip(key, part):
    return filing_plan(key)[1]


def level_of(stream_key, dims, pieces, low, largest):
    gain = 1.0
    for axis_at, parts in pieces:
        steps = jax.random.uniform(jax.random.fold_in(jax.random.fold_in(stream_key, 6), axis_at), (parts,), jnp.float32, low / len(pieces), largest / len(pieces))
        gain = gain * jnp.repeat(jnp.exp(steps), dims[axis_at] // parts).reshape((-1,) + (1,) * (len(dims) - 1 - axis_at))
    return gain


def gaussian(stream_key, extent, deviation, limit, cuts=(), held_as=jnp.bfloat16):
    entries = jax.random.normal(stream_key, extent, jnp.float32) * deviation
    if len(cuts) > 0:
        entries = level_of(stream_key, extent, cuts, -0.22, 0.18) * entries
    return jnp.clip(entries, min=-limit, max=limit).astype(held_as)


def setup_inputs(seed: int = 0) -> dict:
    keys = jax.random.split(jax.random.key(seed), 6)
    return {
        "factors": gaussian(keys[0], (TRACK_BLOCKS, 2, JAC_ROWS, CAM_PARAMS), (JAC_ROWS * TRACK_BLOCKS_DEV // 8) ** -0.5, 0.5, ((0, 256),), jnp.float32),
        "track_clusters": draw_track_clusters(jax.random.fold_in(keys[5], 71), 0),
        "filed_flip": draw_filed_flip(jax.random.fold_in(keys[5], 71), 0),
        "damping": jnp.clip(jnp.exp(math.log(500.0) - 2.3025851 * jax.random.uniform(keys[3], (CLUSTERS, CAM_PARAMS), jnp.float32) ** level_of(keys[3], (CLUSTERS, CAM_PARAMS), ((0, 8),), -0.2, 0.2)), 50.0, 500.0),
        "rhs": gaussian(keys[4], (CLUSTERS, CAM_PARAMS), 500, 3000.0, ((0, 8),), jnp.float32),
    }


highest = lax.Precision.HIGHEST


def apply_system(direction, low_side, high_side, low_cluster, high_cluster, damping):
    low_proj = jnp.einsum("mkc,mc->mk", low_side, direction[low_cluster], precision=highest)
    high_proj = jnp.einsum("mkc,mc->mk", high_side, direction[high_cluster], precision=highest)
    combined = low_proj + high_proj
    low_back = jnp.einsum("mk,mkc->mc", combined, low_side, precision=highest)
    high_back = jnp.einsum("mk,mkc->mc", combined, high_side, precision=highest)
    gathered = jax.ops.segment_sum(low_back, low_cluster, num_segments=CLUSTERS)
    gathered = gathered + jax.ops.segment_sum(high_back, high_cluster, num_segments=CLUSTERS)
    return damping * direction + gathered


def file_blocks(factors, low_cluster, high_cluster, filed_flip):
    flipped = filed_flip == 1
    filed_row = jnp.where(flipped, high_cluster, low_cluster)
    filed_col = jnp.where(flipped, low_cluster, high_cluster)
    oriented = jnp.where(flipped[:, None, None, None], factors[:, ::-1], factors)

    def add_one(item_index, blocks_sum):
        gram_piece = jnp.dot(oriented[item_index, 0].T, oriented[item_index, 1], precision=highest, preferred_element_type=jnp.float32)
        return blocks_sum.at[filed_row[item_index], filed_col[item_index]].add(gram_piece)

    empty = jnp.zeros((CLUSTERS, CLUSTERS, CAM_PARAMS, CAM_PARAMS), jnp.float32)
    return lax.fori_loop(0, TRACK_BLOCKS, add_one, empty)


def reference(factors, track_clusters, filed_flip, damping, rhs):
    low_cluster = track_clusters[:, 0]
    high_cluster = track_clusters[:, 1]
    low_side = factors[:, 0]
    high_side = factors[:, 1]
    precond = damping + jax.ops.segment_sum(jnp.sum(low_side * low_side, axis=1), low_cluster, num_segments=CLUSTERS)
    precond = precond + jax.ops.segment_sum(jnp.sum(high_side * high_side, axis=1), high_cluster, num_segments=CLUSTERS)
    solution = jnp.zeros_like(rhs)
    residual = rhs
    scaled = residual / precond
    direction = scaled
    fitness = jnp.sum(residual * scaled)
    for iteration in range(ITERS):
        images = apply_system(direction, low_side, high_side, low_cluster, high_cluster, damping)
        step_size = fitness / jnp.sum(direction * images)
        solution = solution + step_size * direction
        residual = residual - step_size * images
        scaled = residual / precond
        fitness_next = jnp.sum(residual * scaled)
        direction = scaled + (fitness_next / fitness) * direction
        fitness = fitness_next
    return solution, scaled, file_blocks(factors, low_cluster, high_cluster, filed_flip)
```

```python
import functools

import jax
import jax.numpy as jnp
from jax import lax
from jax.experimental import pallas as pl
from jax.experimental.pallas import tpu as pltpu
from jax.sharding import PartitionSpec as P

CAPACITY = 3
LANES = 128
PACK_STEPS = 8
GRAM_STEPS = 3

VMEM = pl.BlockSpec(memory_space=pltpu.VMEM)
SMEM = pl.BlockSpec(memory_space=pltpu.SMEM)


def tree_sum(parts):
    while len(parts) > 1:
        parts = [parts[at] + parts[at + 1] for at in range(0, len(parts), 2)]
    return parts[0]


def exchange(copies, axis):
    return lax.all_to_all(copies, axis, 0, 0, tiled=True)


def gathered_sum(ref):
    return tree_sum([ref[at] for at in range(ref.shape[0])])


def relay_kernel(in_ref, out_ref):
    out_ref[...] = jnp.broadcast_to(gathered_sum(in_ref)[None], out_ref.shape)


def relay(gathered, copies):
    shape = (copies,) + gathered.shape[1:]
    return pl.pallas_call(
        relay_kernel,
        out_shape=jax.ShapeDtypeStruct(shape, jnp.float32),
        in_specs=[VMEM],
        out_specs=VMEM,
        name="relay",
    )(gathered)


def sum_over_planes(value):
    planes = lax.axis_size("col")
    hop = 1
    while hop < planes:
        pairs = [(at, at ^ hop) for at in range(planes)]
        value = value + lax.ppermute(value, "col", pairs)
        hop *= 2
    return value


def pack_kernel(parity, tracks, clusters_ref, flip_ref, factors_ref, out_ref, counts, slots):
    step = pl.program_id(0)
    blocks, _, jac_rows, params = factors_ref.shape
    per_step = out_ref.shape[0]
    whole = params // LANES * LANES
    pairs = counts.shape[0]
    row_pairs = 2 * tracks

    @pl.when(step == 0)
    def _():
        def clear(pair, carry):
            counts[pair] = 0
            for place in range(CAPACITY):
                slots[pair * CAPACITY + place] = -1
            return carry

        lax.fori_loop(0, pairs, clear, 0, unroll=4)

        def assign(block, carry):
            flip = flip_ref[block]
            low = clusters_ref[0, block]
            high = clusters_ref[1, block]
            first = jnp.where(flip == 1, high, low)
            second = jnp.where(flip == 1, low, high)
            pair = first * row_pairs + second
            place = counts[pair]
            counts[pair] = place + 1
            slots[pair * CAPACITY + place] = block
            return carry

        lax.fori_loop(0, blocks, assign, 0, unroll=4)

    for local in range(per_step):
        for place in range(CAPACITY):
            pair = (step * per_step + local) * 2 + parity
            block = slots[pair * CAPACITY + place]

            @pl.when(block >= 0)
            def _():
                flip = flip_ref[block]
                first = factors_ref[block, flip]
                second = factors_ref[block, 1 - flip]
                out_ref[local, place, :, 0:whole] = first[:, 0:whole]
                out_ref[local, place, :, whole : whole + LANES] = jnp.concatenate(
                    [first[:, whole:params], second[:, whole:params]], axis=1
                )
                out_ref[local, place, :, whole + LANES : 2 * params] = second[:, 0:whole]

            @pl.when(block < 0)
            def _():
                out_ref[local, place] = jnp.zeros((jac_rows, 2 * params), jnp.float32)


def pack(factors, track_clusters, filed_flip, parity, rows, tracks):
    jac_rows, params = factors.shape[2:]
    shape = (rows * tracks, CAPACITY, jac_rows, 2 * params)
    pairs = 2 * rows * tracks
    return pl.pallas_call(
        functools.partial(pack_kernel, parity, tracks),
        grid=(PACK_STEPS,),
        out_shape=jax.ShapeDtypeStruct(shape, jnp.float32),
        in_specs=[
            SMEM,
            SMEM,
            pl.BlockSpec(factors.shape, lambda step: (0, 0, 0, 0)),
        ],
        out_specs=pl.BlockSpec(
            (shape[0] // PACK_STEPS,) + shape[1:], lambda step: (step, 0, 0, 0)
        ),
        scratch_shapes=[
            pltpu.SMEM((pairs,), jnp.int32),
            pltpu.SMEM((pairs * CAPACITY,), jnp.int32),
        ],
        cost_estimate=pl.CostEstimate(
            flops=0,
            bytes_accessed=4 * (factors.size + shape[0] * CAPACITY * jac_rows * 2 * params),
            transcendentals=0,
        ),
        name="pack",
    )(track_clusters, filed_flip, factors)


def gram_kernel(params, in_ref, out_ref, total):
    step = pl.program_id(0)
    whole = params // LANES * LANES
    wide = whole + LANES
    value = in_ref[...]
    high = value.astype(jnp.bfloat16)
    low = (value - high.astype(jnp.float32)).astype(jnp.bfloat16)
    product = functools.partial(
        lax.dot_general,
        dimension_numbers=(((0,), (0,)), ((), ())),
        preferred_element_type=jnp.float32,
    )
    first, second = slice(0, wide), slice(whole, 2 * params)
    gram = product(high[:, first], high[:, second])
    gram = gram + product(high[:, first], low[:, second])
    gram = gram + product(low[:, first], high[:, second])

    @pl.when(step == 0)
    def _():
        total[...] = gram

    @pl.when(step > 0)
    def _():
        total[...] += gram

    @pl.when(step == pl.num_programs(0) - 1)
    def _():
        out_ref[:, 0:whole] = total[0:params, LANES:wide]
        out_ref[:, whole:params] = total[0:params, params - whole : LANES]


def gram(received, params):
    received = received.reshape(-1, 2 * params)
    rows, width = received.shape
    wide = params // LANES * LANES + LANES
    return pl.pallas_call(
        functools.partial(gram_kernel, params),
        grid=(GRAM_STEPS,),
        out_shape=jax.ShapeDtypeStruct((params, params), jnp.float32),
        in_specs=[pl.BlockSpec((rows // GRAM_STEPS, width), lambda step: (step, 0))],
        out_specs=pl.BlockSpec((params, params), lambda step: (0, 0)),
        scratch_shapes=[pltpu.VMEM((wide, wide), jnp.float32)],
        cost_estimate=pl.CostEstimate(
            flops=6 * rows * wide * wide,
            bytes_accessed=4 * (rows * width + params * params),
            transcendentals=0,
        ),
        name="gram",
    )(received)


def plane_rows(block):
    return lax.psum_scatter(block, "col", scatter_dimension=0, tiled=True)


def placed(piece, parity):
    n_col = lax.axis_size("col")
    n_track = lax.axis_size("track")
    halves = n_col // n_track
    out = []
    for half in range(halves):
        moves = []
        for col in range(half, n_col, halves):
            for track in range(n_track):
                target = (2 * track + parity) * n_track + col // halves
                moves.append((col * n_track + track, target))
        out.append(lax.ppermute(piece, ("col", "track"), moves))
    return jnp.concatenate(out, axis=0)


def diag_kernel(clusters_ref, factors_ref, damping_ref, rhs_ref, out_ref, sums):
    blocks, sides, _, params = factors_ref.shape
    clusters = sums.shape[0]
    sums[...] = jnp.zeros_like(sums)

    def add_block(block, carry):
        for side in range(sides):
            value = factors_ref[block, side]
            squares = value * value
            sums[clusters_ref[side, block]] += squares[0:8] + squares[8:16]
        return carry

    lax.fori_loop(0, blocks, add_block, 0, unroll=4)
    for at in range(clusters):
        total = jnp.sum(sums[at], axis=0, keepdims=True)
        for copy in range(out_ref.shape[0]):
            out_ref[copy, at : at + 1] = total
    ids = lax.broadcasted_iota(jnp.int32, (clusters, params), 0)
    damping = jnp.broadcast_to(damping_ref[...], (clusters, params))
    rhs = jnp.broadcast_to(rhs_ref[...], (clusters, params))
    for copy in range(out_ref.shape[0]):
        out_ref[copy, clusters:] = jnp.where(ids == 0, damping, rhs)


def settle_kernel(in_ref, out_ref, vectors_ref):
    clusters = vectors_ref.shape[1]
    total = tree_sum([in_ref[at, 0:clusters] for at in range(in_ref.shape[0])])
    out_ref[...] = jnp.broadcast_to(total[None], out_ref.shape)
    for at in range(clusters):
        vectors_ref[0, at : at + 1] = in_ref[at, clusters : clusters + 1]
        vectors_ref[1, at : at + 1] = in_ref[at, clusters + 1 : clusters + 2]


def system_part(clusters_ref, factors_ref, direction, spread, sums):
    blocks = factors_ref.shape[0]
    clusters, params = direction.shape
    sums[...] = jnp.zeros_like(sums)
    for at in range(clusters):
        spread[at] = jnp.broadcast_to(direction[at : at + 1], (8, params))

    def add_block(block, carry):
        low = clusters_ref[0, block]
        high = clusters_ref[1, block]
        low_side = [factors_ref[block, 0, 0:8], factors_ref[block, 0, 8:16]]
        high_side = [factors_ref[block, 1, 0:8], factors_ref[block, 1, 8:16]]
        low_dir = spread[low]
        high_dir = spread[high]
        projected = [
            jnp.sum(one * low_dir + two * high_dir, axis=1, keepdims=True)
            for one, two in zip(low_side, high_side)
        ]
        sums[low] += low_side[0] * projected[0] + low_side[1] * projected[1]
        sums[high] += high_side[0] * projected[0] + high_side[1] * projected[1]
        return carry

    lax.fori_loop(0, blocks, add_block, 0, unroll=8)
    return [jnp.sum(sums[at], axis=0, keepdims=True) for at in range(clusters)]


def total_of(value):
    return jnp.sum(jnp.sum(value, axis=1, keepdims=True), axis=0, keepdims=True)


def begin_kernel(
    clusters_ref, factors_ref, vectors_ref, diag_ref, part_ref, state_ref, spread, sums
):
    damping = vectors_ref[0]
    residual = vectors_ref[1]
    precond = damping + diag_ref[...]
    direction = residual / precond
    state_ref[0] = damping
    state_ref[1] = precond
    state_ref[2] = jnp.zeros_like(residual)
    state_ref[3] = residual
    state_ref[4] = direction
    parts = system_part(clusters_ref, factors_ref, direction, spread, sums)
    for at, part in enumerate(parts):
        part_ref[at : at + 1] = part


def iterate_kernel(
    clusters_ref, factors_ref, state_ref, images_ref, part_ref, out_ref, spread, sums
):
    damping, precond, solution, residual, direction = [state_ref[at] for at in range(5)]
    images = gathered_sum(images_ref) + damping * direction
    fitness = total_of(residual * (residual / precond))
    step_size = fitness / total_of(direction * images)
    solution = solution + step_size * direction
    residual = residual - step_size * images
    scaled = residual / precond
    fitness_next = total_of(residual * scaled)
    direction = scaled + fitness_next / fitness * direction
    out_ref[0] = damping
    out_ref[1] = precond
    out_ref[2] = solution
    out_ref[3] = residual
    out_ref[4] = direction
    parts = system_part(clusters_ref, factors_ref, direction, spread, sums)
    curvature = sum(
        jnp.sum(direction[at : at + 1] * part, axis=1, keepdims=True)
        for at, part in enumerate(parts)
    )
    curvature = jnp.broadcast_to(curvature, parts[0].shape)
    tracks = part_ref.shape[0] // len(parts)
    for at, part in enumerate(parts):
        for track in range(tracks):
            part_ref[at * tracks + track, 0:1] = part
            part_ref[at * tracks + track, 1:2] = curvature


def finish_kernel(place_ref, state_ref, images_ref, solution_ref, scaled_ref, rows):
    damping, precond, _, residual, direction = [state_ref[at] for at in range(5)]
    for vector in range(5):
        for at in range(damping.shape[0]):
            rows[vector, at] = state_ref[vector, at : at + 1]
    row = place_ref[0]
    own = gathered_sum(images_ref)
    images = own[0:1] + rows[0, row] * rows[4, row]
    curvature = own[1:2, 0:1] + total_of(damping * direction * direction)
    step_size = total_of(residual * (residual / precond)) / curvature
    solution_ref[...] = rows[2, row] + step_size * rows[4, row]
    scaled_ref[...] = (rows[3, row] - step_size * images) / rows[1, row]


def on_device(factors, track_clusters, filed_flip, damping, rhs):
    n_row = lax.axis_size("row")
    n_col = lax.axis_size("col")
    n_track = lax.axis_size("track")
    params = factors.shape[3]
    clusters = n_row
    track_clusters = track_clusters.T
    spread = pltpu.VMEM((clusters, 8, params), jnp.float32)
    state_shape = jax.ShapeDtypeStruct((5, clusters, params), jnp.float32)

    def shape_of(*shape):
        return jax.ShapeDtypeStruct(shape, jnp.float32)

    squares = pl.pallas_call(
        diag_kernel,
        out_shape=shape_of(n_row, 2 * clusters, params),
        in_specs=[SMEM, VMEM, VMEM, VMEM],
        out_specs=VMEM,
        scratch_shapes=[spread],
        name="diag",
    )(track_clusters, factors, damping, rhs)
    even = pack(factors, track_clusters, filed_flip, 0, n_row, n_track)
    squares, vectors = pl.pallas_call(
        settle_kernel,
        out_shape=(shape_of(n_track, clusters, params), shape_of(2, clusters, params)),
        in_specs=[VMEM],
        out_specs=(VMEM, VMEM),
        name="settle",
    )(exchange(squares, "row"))
    squares = relay(exchange(squares, "track"), 1)[0]

    even, squares = lax.optimization_barrier((even, squares))
    even = exchange(even, ("row", "track"))
    part, state = pl.pallas_call(
        begin_kernel,
        out_shape=(shape_of(clusters, params), state_shape),
        in_specs=[SMEM] + [VMEM] * 3,
        out_specs=(VMEM, VMEM),
        scratch_shapes=[spread, spread],
        name="begin",
    )(track_clusters, factors, vectors, sum_over_planes(squares))
    part = sum_over_planes(part)
    part = jnp.broadcast_to(part[None], (n_row * n_track,) + part.shape)
    odd = pack(factors, track_clusters, filed_flip, 1, n_row, n_track)
    odd, part, state = lax.optimization_barrier((odd, part, state))
    odd = exchange(odd, ("row", "track"))
    block = gram(even, params)
    even_out = placed(plane_rows(block), 0)
    odd, part, block = lax.optimization_barrier((odd, part, block))
    piece = plane_rows(gram(odd, params))

    part, state = pl.pallas_call(
        iterate_kernel,
        out_shape=(shape_of(n_row * n_track, 2, params), state_shape),
        in_specs=[SMEM] + [VMEM] * 3,
        out_specs=(VMEM, VMEM),
        scratch_shapes=[spread, spread],
        name="iterate",
    )(track_clusters, factors, state, exchange(part, ("row", "track")))
    part = exchange(relay(exchange(part, ("row", "track")), n_col), "col")
    piece, part = lax.optimization_barrier((piece, part))
    odd_out = placed(piece, 1)
    row_id = lax.axis_index("row").astype(jnp.int32).reshape(1)
    solution_out, scaled = pl.pallas_call(
        finish_kernel,
        out_shape=(shape_of(1, params), shape_of(1, params)),
        in_specs=[SMEM, VMEM, VMEM],
        out_specs=(VMEM, VMEM),
        scratch_shapes=[pltpu.VMEM((5, clusters, 1, params), jnp.float32)],
        name="finish",
    )(row_id, state, part)
    return solution_out, scaled, (even_out + odd_out)[None, None]


def solution(mesh):
    in_specs = (
        P(("row", "col", "track"), None, None, None),
        P(("row", "col", "track"), None),
        P(("row", "col", "track")),
        P("row", None),
        P("row", None),
    )
    out_specs = (P("row", None), P("row", None), P("row", "col", "track", None))
    return jax.shard_map(
        on_device, mesh=mesh, in_specs=in_specs, out_specs=out_specs, check_vma=False
    )
```

```python
import functools

import jax
import jax.numpy as jnp
from jax import lax
from jax.experimental import pallas as pl
from jax.experimental.pallas import tpu as pltpu
from jax.sharding import PartitionSpec as P

CAPACITY = 3
LANES = 128
PACK_STEPS = 8
GRAM_STEPS = 3

VMEM = pl.BlockSpec(memory_space=pltpu.VMEM)
SMEM = pl.BlockSpec(memory_space=pltpu.SMEM)


def tree_sum(parts):
    while len(parts) > 1:
        parts = [parts[at] + parts[at + 1] for at in range(0, len(parts), 2)]
    return parts[0]


def exchange(copies, axis):
    return lax.all_to_all(copies, axis, 0, 0, tiled=True)


def gathered_sum(ref):
    return tree_sum([ref[at] for at in range(ref.shape[0])])


def relay_kernel(in_ref, out_ref):
    out_ref[...] = jnp.broadcast_to(gathered_sum(in_ref)[None], out_ref.shape)


def relay(gathered, copies):
    shape = (copies,) + gathered.shape[1:]
    return pl.pallas_call(
        relay_kernel,
        out_shape=jax.ShapeDtypeStruct(shape, jnp.float32),
        in_specs=[VMEM],
        out_specs=VMEM,
        name="relay",
    )(gathered)


def sum_over_planes(value):
    planes = lax.axis_size("col")
    hop = 1
    while hop < planes:
        pairs = [(at, at ^ hop) for at in range(planes)]
        value = value + lax.ppermute(value, "col", pairs)
        hop *= 2
    return value


def pack_kernel(parity, tracks, clusters_ref, flip_ref, factors_ref, out_ref, counts, slots):
    step = pl.program_id(0)
    blocks, _, jac_rows, params = factors_ref.shape
    per_step = out_ref.shape[0]
    whole = params // LANES * LANES
    pairs = counts.shape[0]
    row_pairs = 2 * tracks

    @pl.when(step == 0)
    def _():
        def clear(pair, carry):
            counts[pair] = 0
            for place in range(CAPACITY):
                slots[pair * CAPACITY + place] = -1
            return carry

        lax.fori_loop(0, pairs, clear, 0, unroll=4)

        def assign(block, carry):
            flip = flip_ref[block]
            low = clusters_ref[0, block]
            high = clusters_ref[1, block]
            first = jnp.where(flip == 1, high, low)
            second = jnp.where(flip == 1, low, high)
            pair = first * row_pairs + second
            place = counts[pair]
            counts[pair] = place + 1
            slots[pair * CAPACITY + place] = block
            return carry

        lax.fori_loop(0, blocks, assign, 0, unroll=4)

    for local in range(per_step):
        for place in range(CAPACITY):
            pair = (step * per_step + local) * 2 + parity
            block = slots[pair * CAPACITY + place]

            @pl.when(block >= 0)
            def _():
                flip = flip_ref[block]
                first = factors_ref[block, flip]
                second = factors_ref[block, 1 - flip]
                out_ref[local, place, :, 0:whole] = first[:, 0:whole]
                out_ref[local, place, :, whole : whole + LANES] = jnp.concatenate(
                    [first[:, whole:params], second[:, whole:params]], axis=1
                )
                out_ref[local, place, :, whole + LANES : 2 * params] = second[:, 0:whole]

            @pl.when(block < 0)
            def _():
                out_ref[local, place] = jnp.zeros((jac_rows, 2 * params), jnp.float32)


def pack(factors, track_clusters, filed_flip, parity, rows, tracks):
    jac_rows, params = factors.shape[2:]
    shape = (rows * tracks, CAPACITY, jac_rows, 2 * params)
    pairs = 2 * rows * tracks
    return pl.pallas_call(
        functools.partial(pack_kernel, parity, tracks),
        grid=(PACK_STEPS,),
        out_shape=jax.ShapeDtypeStruct(shape, jnp.float32),
        in_specs=[
            SMEM,
            SMEM,
            pl.BlockSpec(factors.shape, lambda step: (0, 0, 0, 0)),
        ],
        out_specs=pl.BlockSpec(
            (shape[0] // PACK_STEPS,) + shape[1:], lambda step: (step, 0, 0, 0)
        ),
        scratch_shapes=[
            pltpu.SMEM((pairs,), jnp.int32),
            pltpu.SMEM((pairs * CAPACITY,), jnp.int32),
        ],
        cost_estimate=pl.CostEstimate(
            flops=0,
            bytes_accessed=4 * (factors.size + shape[0] * CAPACITY * jac_rows * 2 * params),
            transcendentals=0,
        ),
        name="pack",
    )(track_clusters, filed_flip, factors)


def gram_kernel(params, in_ref, out_ref, total):
    step = pl.program_id(0)
    whole = params // LANES * LANES
    wide = whole + LANES
    value = in_ref[...]
    high = value.astype(jnp.bfloat16)
    low = (value - high.astype(jnp.float32)).astype(jnp.bfloat16)
    product = functools.partial(
        lax.dot_general,
        dimension_numbers=(((0,), (0,)), ((), ())),
        preferred_element_type=jnp.float32,
    )
    first, second = slice(0, wide), slice(whole, 2 * params)
    gram = product(high[:, first], high[:, second])
    gram = gram + product(high[:, first], low[:, second])
    gram = gram + product(low[:, first], high[:, second])

    @pl.when(step == 0)
    def _():
        total[...] = gram

    @pl.when(step > 0)
    def _():
        total[...] += gram

    @pl.when(step == pl.num_programs(0) - 1)
    def _():
        out_ref[:, 0:whole] = total[0:params, LANES:wide]
        out_ref[:, whole:params] = total[0:params, params - whole : LANES]


def gram(received, params):
    received = received.reshape(-1, 2 * params)
    rows, width = received.shape
    wide = params // LANES * LANES + LANES
    return pl.pallas_call(
        functools.partial(gram_kernel, params),
        grid=(GRAM_STEPS,),
        out_shape=jax.ShapeDtypeStruct((params, params), jnp.float32),
        in_specs=[pl.BlockSpec((rows // GRAM_STEPS, width), lambda step: (step, 0))],
        out_specs=pl.BlockSpec((params, params), lambda step: (0, 0)),
        scratch_shapes=[pltpu.VMEM((wide, wide), jnp.float32)],
        cost_estimate=pl.CostEstimate(
            flops=6 * rows * wide * wide,
            bytes_accessed=4 * (rows * width + params * params),
            transcendentals=0,
        ),
        name="gram",
    )(received)


def plane_rows(block):
    return lax.psum_scatter(block, "col", scatter_dimension=0, tiled=True)


def placed(piece, parity):
    n_col = lax.axis_size("col")
    n_track = lax.axis_size("track")
    halves = n_col // n_track
    out = []
    for half in range(halves):
        moves = []
        for col in range(half, n_col, halves):
            for track in range(n_track):
                target = (2 * track + parity) * n_track + col // halves
                moves.append((col * n_track + track, target))
        out.append(lax.ppermute(piece, ("col", "track"), moves))
    return jnp.concatenate(out, axis=0)


def diag_kernel(clusters_ref, factors_ref, damping_ref, rhs_ref, out_ref, sums):
    blocks, sides, _, params = factors_ref.shape
    clusters = sums.shape[0]
    sums[...] = jnp.zeros_like(sums)

    def add_block(block, carry):
        for side in range(sides):
            value = factors_ref[block, side]
            squares = value * value
            sums[clusters_ref[side, block]] += squares[0:8] + squares[8:16]
        return carry

    lax.fori_loop(0, blocks, add_block, 0, unroll=4)
    for at in range(clusters):
        total = jnp.sum(sums[at], axis=0, keepdims=True)
        for copy in range(out_ref.shape[0]):
            out_ref[copy, at : at + 1] = total
    ids = lax.broadcasted_iota(jnp.int32, (clusters, params), 0)
    damping = jnp.broadcast_to(damping_ref[...], (clusters, params))
    rhs = jnp.broadcast_to(rhs_ref[...], (clusters, params))
    for copy in range(out_ref.shape[0]):
        out_ref[copy, clusters:] = jnp.where(ids == 0, damping, rhs)


def settle_kernel(in_ref, out_ref, vectors_ref):
    clusters = vectors_ref.shape[1]
    total = tree_sum([in_ref[at, 0:clusters] for at in range(in_ref.shape[0])])
    out_ref[...] = jnp.broadcast_to(total[None], out_ref.shape)
    for at in range(clusters):
        vectors_ref[0, at : at + 1] = in_ref[at, clusters : clusters + 1]
        vectors_ref[1, at : at + 1] = in_ref[at, clusters + 1 : clusters + 2]


def system_part(clusters_ref, factors_ref, direction, spread, sums):
    blocks = factors_ref.shape[0]
    clusters, params = direction.shape
    sums[...] = jnp.zeros_like(sums)
    for at in range(clusters):
        spread[at] = jnp.broadcast_to(direction[at : at + 1], (8, params))

    def add_block(block, carry):
        low = clusters_ref[0, block]
        high = clusters_ref[1, block]
        low_side = [factors_ref[block, 0, 0:8], factors_ref[block, 0, 8:16]]
        high_side = [factors_ref[block, 1, 0:8], factors_ref[block, 1, 8:16]]
        low_dir = spread[low]
        high_dir = spread[high]
        projected = [
            jnp.sum(one * low_dir + two * high_dir, axis=1, keepdims=True)
            for one, two in zip(low_side, high_side)
        ]
        sums[low] += low_side[0] * projected[0] + low_side[1] * projected[1]
        sums[high] += high_side[0] * projected[0] + high_side[1] * projected[1]
        return carry

    lax.fori_loop(0, blocks, add_block, 0, unroll=8)
    return [jnp.sum(sums[at], axis=0, keepdims=True) for at in range(clusters)]


def total_of(value):
    return jnp.sum(jnp.sum(value, axis=1, keepdims=True), axis=0, keepdims=True)


def begin_kernel(
    clusters_ref, factors_ref, vectors_ref, diag_ref, part_ref, state_ref, spread, sums
):
    damping = vectors_ref[0]
    residual = vectors_ref[1]
    precond = damping + diag_ref[...]
    direction = residual / precond
    state_ref[0] = damping
    state_ref[1] = precond
    state_ref[2] = jnp.zeros_like(residual)
    state_ref[3] = residual
    state_ref[4] = direction
    parts = system_part(clusters_ref, factors_ref, direction, spread, sums)
    for at, part in enumerate(parts):
        part_ref[at : at + 1] = part


def iterate_kernel(
    clusters_ref, factors_ref, state_ref, images_ref, part_ref, out_ref, spread, sums
):
    damping, precond, solution, residual, direction = [state_ref[at] for at in range(5)]
    images = gathered_sum(images_ref) + damping * direction
    fitness = total_of(residual * (residual / precond))
    step_size = fitness / total_of(direction * images)
    solution = solution + step_size * direction
    residual = residual - step_size * images
    scaled = residual / precond
    fitness_next = total_of(residual * scaled)
    direction = scaled + fitness_next / fitness * direction
    out_ref[0] = damping
    out_ref[1] = precond
    out_ref[2] = solution
    out_ref[3] = residual
    out_ref[4] = direction
    parts = system_part(clusters_ref, factors_ref, direction, spread, sums)
    curvature = sum(
        jnp.sum(direction[at : at + 1] * part, axis=1, keepdims=True)
        for at, part in enumerate(parts)
    )
    curvature = jnp.broadcast_to(curvature, parts[0].shape)
    tracks = part_ref.shape[0] // len(parts)
    for at, part in enumerate(parts):
        for track in range(tracks):
            part_ref[at * tracks + track, 0:1] = part
            part_ref[at * tracks + track, 1:2] = curvature


def finish_kernel(place_ref, state_ref, images_ref, solution_ref, scaled_ref, rows):
    damping, precond, _, residual, direction = [state_ref[at] for at in range(5)]
    for vector in range(5):
        for at in range(damping.shape[0]):
            rows[vector, at] = state_ref[vector, at : at + 1]
    row = place_ref[0]
    own = gathered_sum(images_ref)
    images = own[0:1] + rows[0, row] * rows[4, row]
    curvature = own[1:2, 0:1] + total_of(damping * direction * direction)
    step_size = total_of(residual * (residual / precond)) / curvature
    solution_ref[...] = rows[2, row] + step_size * rows[4, row]
    scaled_ref[...] = (rows[3, row] - step_size * images) / rows[1, row]


def on_device(factors, track_clusters, filed_flip, damping, rhs):
    n_row = lax.axis_size("row")
    n_col = lax.axis_size("col")
    n_track = lax.axis_size("track")
    params = factors.shape[3]
    clusters = n_row
    track_clusters = track_clusters.T
    spread = pltpu.VMEM((clusters, 8, params), jnp.float32)
    state_shape = jax.ShapeDtypeStruct((5, clusters, params), jnp.float32)

    def shape_of(*shape):
        return jax.ShapeDtypeStruct(shape, jnp.float32)

    squares = pl.pallas_call(
        diag_kernel,
        out_shape=shape_of(n_row, 2 * clusters, params),
        in_specs=[SMEM, VMEM, VMEM, VMEM],
        out_specs=VMEM,
        scratch_shapes=[spread],
        name="diag",
    )(track_clusters, factors, damping, rhs)
    even = pack(factors, track_clusters, filed_flip, 0, n_row, n_track)
    squares, vectors = pl.pallas_call(
        settle_kernel,
        out_shape=(shape_of(n_track, clusters, params), shape_of(2, clusters, params)),
        in_specs=[VMEM],
        out_specs=(VMEM, VMEM),
        name="settle",
    )(exchange(squares, "row"))
    squares = relay(exchange(squares, "track"), 1)[0]

    even, squares = lax.optimization_barrier((even, squares))
    even = exchange(even, ("row", "track"))
    part, state = pl.pallas_call(
        begin_kernel,
        out_shape=(shape_of(clusters, params), state_shape),
        in_specs=[SMEM] + [VMEM] * 3,
        out_specs=(VMEM, VMEM),
        scratch_shapes=[spread, spread],
        name="begin",
    )(track_clusters, factors, vectors, sum_over_planes(squares))
    part = sum_over_planes(part)
    part = jnp.broadcast_to(part[None], (n_row * n_track,) + part.shape)
    odd = pack(factors, track_clusters, filed_flip, 1, n_row, n_track)
    odd, part, state = lax.optimization_barrier((odd, part, state))
    odd = exchange(odd, ("row", "track"))
    block = gram(even, params)
    even_out = placed(plane_rows(block), 0)
    odd, part, block = lax.optimization_barrier((odd, part, block))
    piece = plane_rows(gram(odd, params))

    part, state = pl.pallas_call(
        iterate_kernel,
        out_shape=(shape_of(n_row * n_track, 2, params), state_shape),
        in_specs=[SMEM] + [VMEM] * 3,
        out_specs=(VMEM, VMEM),
        scratch_shapes=[spread, spread],
        name="iterate",
    )(track_clusters, factors, state, exchange(part, ("row", "track")))
    part = relay(exchange(part, ("row", "track")), n_col)
    part, even_out = lax.optimization_barrier((part, even_out))
    part = exchange(part, "col")
    piece, part = lax.optimization_barrier((piece, part))
    odd_out = placed(piece, 1)
    row_id = lax.axis_index("row").astype(jnp.int32).reshape(1)
    solution_out, scaled = pl.pallas_call(
        finish_kernel,
        out_shape=(shape_of(1, params), shape_of(1, params)),
        in_specs=[SMEM, VMEM, VMEM],
        out_specs=(VMEM, VMEM),
        scratch_shapes=[pltpu.VMEM((5, clusters, 1, params), jnp.float32)],
        name="finish",
    )(row_id, state, part)
    return solution_out, scaled, (even_out + odd_out)[None, None]


def solution(mesh):
    in_specs = (
        P(("row", "col", "track"), None, None, None),
        P(("row", "col", "track"), None),
        P(("row", "col", "track")),
        P("row", None),
        P("row", None),
    )
    out_specs = (P("row", None), P("row", None), P("row", "col", "track", None))
    return jax.shard_map(
        on_device, mesh=mesh, in_specs=in_specs, out_specs=out_specs, check_vma=False
    )
```

```python
import functools

import jax
import jax.numpy as jnp
from jax import lax
from jax.experimental import pallas as pl
from jax.experimental.pallas import tpu as pltpu
from jax.sharding import PartitionSpec as P

CAPACITY = 3
LANES = 128
PACK_STEPS = 8
EARLY = ((0, 0), (0, 1), (0, 2), (1, 0), (1, 1))
LATE = ((1, 2),)

VMEM = pl.BlockSpec(memory_space=pltpu.VMEM)
SMEM = pl.BlockSpec(memory_space=pltpu.SMEM)


def tree_sum(parts):
    while len(parts) > 1:
        parts = [parts[at] + parts[at + 1] for at in range(0, len(parts), 2)]
    return parts[0]


def exchange(copies, axis):
    return lax.all_to_all(copies, axis, 0, 0, tiled=True)


def gathered_sum(ref):
    return tree_sum([ref[at] for at in range(ref.shape[0])])


def relay_kernel(in_ref, out_ref):
    out_ref[...] = jnp.broadcast_to(gathered_sum(in_ref)[None], out_ref.shape)


def relay(gathered, copies):
    shape = (copies,) + gathered.shape[1:]
    return pl.pallas_call(
        relay_kernel,
        out_shape=jax.ShapeDtypeStruct(shape, jnp.float32),
        in_specs=[VMEM],
        out_specs=VMEM,
        name="relay",
    )(gathered)


def sum_over_planes(value):
    planes = lax.axis_size("col")
    hop = 1
    while hop < planes:
        pairs = [(at, at ^ hop) for at in range(planes)]
        value = value + lax.ppermute(value, "col", pairs)
        hop *= 2
    return value


def pack_kernel(chosen, tracks, clusters_ref, flip_ref, factors_ref, out_ref, counts, slots):
    step = pl.program_id(0)
    blocks, _, jac_rows, params = factors_ref.shape
    per_step = out_ref.shape[0]
    whole = params // LANES * LANES
    pairs = counts.shape[0]
    row_pairs = 2 * tracks

    @pl.when(step == 0)
    def _():
        def clear(pair, carry):
            counts[pair] = 0
            for place in range(CAPACITY):
                slots[pair * CAPACITY + place] = -1
            return carry

        lax.fori_loop(0, pairs, clear, 0, unroll=4)

        def assign(block, carry):
            flip = flip_ref[block]
            low = clusters_ref[0, block]
            high = clusters_ref[1, block]
            first = jnp.where(flip == 1, high, low)
            second = jnp.where(flip == 1, low, high)
            pair = first * row_pairs + second
            place = counts[pair]
            counts[pair] = place + 1
            slots[pair * CAPACITY + place] = block
            return carry

        lax.fori_loop(0, blocks, assign, 0, unroll=4)

    for local in range(per_step):
        for at, (parity, place) in enumerate(chosen):
            pair = (step * per_step + local) * 2 + parity
            block = slots[pair * CAPACITY + place]

            @pl.when(block >= 0)
            def _():
                flip = flip_ref[block]
                first = factors_ref[block, flip]
                second = factors_ref[block, 1 - flip]
                out_ref[local, at, :, 0:whole] = first[:, 0:whole]
                out_ref[local, at, :, whole : whole + LANES] = jnp.concatenate(
                    [first[:, whole:params], second[:, whole:params]], axis=1
                )
                out_ref[local, at, :, whole + LANES : 2 * params] = second[:, 0:whole]

            @pl.when(block < 0)
            def _():
                out_ref[local, at] = jnp.zeros((jac_rows, 2 * params), jnp.float32)


def pack(factors, track_clusters, filed_flip, chosen, rows, tracks):
    jac_rows, params = factors.shape[2:]
    shape = (rows * tracks, len(chosen), jac_rows, 2 * params)
    pairs = 2 * rows * tracks
    return pl.pallas_call(
        functools.partial(pack_kernel, chosen, tracks),
        grid=(PACK_STEPS,),
        out_shape=jax.ShapeDtypeStruct(shape, jnp.float32),
        in_specs=[
            SMEM,
            SMEM,
            pl.BlockSpec(factors.shape, lambda step: (0, 0, 0, 0)),
        ],
        out_specs=pl.BlockSpec(
            (shape[0] // PACK_STEPS,) + shape[1:], lambda step: (step, 0, 0, 0)
        ),
        scratch_shapes=[
            pltpu.SMEM((pairs,), jnp.int32),
            pltpu.SMEM((pairs * CAPACITY,), jnp.int32),
        ],
        cost_estimate=pl.CostEstimate(
            flops=0,
            bytes_accessed=4 * (factors.size + shape[0] * shape[1] * jac_rows * 2 * params),
            transcendentals=0,
        ),
        name="pack",
    )(track_clusters, filed_flip, factors)


def product_of(value, params):
    whole = params // LANES * LANES
    high = value.astype(jnp.bfloat16)
    low = (value - high.astype(jnp.float32)).astype(jnp.bfloat16)
    product = functools.partial(
        lax.dot_general,
        dimension_numbers=(((0,), (0,)), ((), ())),
        preferred_element_type=jnp.float32,
    )
    first, second = slice(0, whole + LANES), slice(whole, 2 * params)
    gram = product(high[:, first], high[:, second])
    gram = gram + product(high[:, first], low[:, second])
    return gram + product(low[:, first], high[:, second])


def plane_of(parity, track, part, planes):
    if parity == 0:
        return (2 * track - part + planes) % planes
    return (2 * track + 1 + part) % planes


def store_parts(out_ref, total, parity, track, params, add=False):
    planes, share = out_ref.shape[:2]
    whole = params // LANES * LANES
    wide = whole + LANES
    for part in range(params // share):
        plane = lax.rem(
            2 * track - part + planes if parity == 0 else 2 * track + 1 + part, planes
        )
        rows = slice(part * share, (part + 1) * share)
        main = total[rows, LANES:wide]
        tail = total[rows, params - whole : LANES]
        if add:
            main = out_ref[plane, :, 0:whole] + main
            tail = out_ref[plane, :, whole:params] + tail
        out_ref[plane, :, 0:whole] = main
        out_ref[plane, :, whole:params] = tail


def early_kernel(params, track_ref, in_ref, out_ref, totals):
    step = pl.program_id(0)
    gram = product_of(in_ref[...].reshape(-1, 2 * params), params)
    for at, (parity, place) in enumerate(EARLY):

        @pl.when(step == at)
        def _():
            if place == 0:
                totals[parity] = gram
            else:
                totals[parity] += gram

    @pl.when(step == pl.num_programs(0) - 1)
    def _():
        for parity in range(2):
            store_parts(out_ref, totals.at[parity], parity, track_ref[0], params)


def late_kernel(params, track_ref, in_ref, blocks_ref, out_ref, total):
    out_ref[...] = blocks_ref[...]
    total[...] = product_of(in_ref[...].reshape(-1, 2 * params), params)
    store_parts(out_ref, total, 1, track_ref[0], params, add=True)


def gram_cost(slots, params):
    return pl.CostEstimate(
        flops=6 * 512 * 640 * 640 * slots,
        bytes_accessed=4 * (512 * 2 * params * slots + 2 * params * params),
        transcendentals=0,
    )


def early_products(track, received, params, planes):
    devices, slots, jac_rows, width = received.shape
    share = 2 * params // planes
    wide = params // LANES * LANES + LANES
    return pl.pallas_call(
        functools.partial(early_kernel, params),
        grid=(slots,),
        out_shape=jax.ShapeDtypeStruct((planes, share, params), jnp.float32),
        in_specs=[
            SMEM,
            pl.BlockSpec((devices, 1, jac_rows, width), lambda step: (0, step, 0, 0)),
        ],
        out_specs=pl.BlockSpec((planes, share, params), lambda step: (0, 0, 0)),
        scratch_shapes=[pltpu.VMEM((2, wide, wide), jnp.float32)],
        cost_estimate=gram_cost(slots, params),
        name="early",
    )(track, received)


def late_products(track, received, blocks, params):
    wide = params // LANES * LANES + LANES
    return pl.pallas_call(
        functools.partial(late_kernel, params),
        out_shape=jax.ShapeDtypeStruct(blocks.shape, jnp.float32),
        in_specs=[SMEM, VMEM, VMEM],
        out_specs=VMEM,
        scratch_shapes=[pltpu.VMEM((wide, wide), jnp.float32)],
        cost_estimate=gram_cost(received.shape[1], params),
        name="late",
    )(track, received, blocks)


def diag_kernel(clusters_ref, factors_ref, damping_ref, rhs_ref, out_ref, sums):
    blocks, sides, _, params = factors_ref.shape
    clusters = sums.shape[0]
    sums[...] = jnp.zeros_like(sums)

    def add_block(block, carry):
        for side in range(sides):
            value = factors_ref[block, side]
            squares = value * value
            sums[clusters_ref[side, block]] += squares[0:8] + squares[8:16]
        return carry

    lax.fori_loop(0, blocks, add_block, 0, unroll=4)
    for at in range(clusters):
        total = jnp.sum(sums[at], axis=0, keepdims=True)
        for copy in range(out_ref.shape[0]):
            out_ref[copy, at : at + 1] = total
    ids = lax.broadcasted_iota(jnp.int32, (clusters, params), 0)
    damping = jnp.broadcast_to(damping_ref[...], (clusters, params))
    rhs = jnp.broadcast_to(rhs_ref[...], (clusters, params))
    for copy in range(out_ref.shape[0]):
        out_ref[copy, clusters:] = jnp.where(ids == 0, damping, rhs)


def settle_kernel(in_ref, out_ref, vectors_ref):
    clusters = vectors_ref.shape[1]
    total = tree_sum([in_ref[at, 0:clusters] for at in range(in_ref.shape[0])])
    out_ref[...] = jnp.broadcast_to(total[None], out_ref.shape)
    for at in range(clusters):
        vectors_ref[0, at : at + 1] = in_ref[at, clusters : clusters + 1]
        vectors_ref[1, at : at + 1] = in_ref[at, clusters + 1 : clusters + 2]


def system_part(clusters_ref, factors_ref, direction, spread, sums):
    blocks = factors_ref.shape[0]
    clusters, params = direction.shape
    sums[...] = jnp.zeros_like(sums)
    for at in range(clusters):
        spread[at] = jnp.broadcast_to(direction[at : at + 1], (8, params))

    def add_block(block, carry):
        low = clusters_ref[0, block]
        high = clusters_ref[1, block]
        low_side = [factors_ref[block, 0, 0:8], factors_ref[block, 0, 8:16]]
        high_side = [factors_ref[block, 1, 0:8], factors_ref[block, 1, 8:16]]
        low_dir = spread[low]
        high_dir = spread[high]
        projected = [
            jnp.sum(one * low_dir + two * high_dir, axis=1, keepdims=True)
            for one, two in zip(low_side, high_side)
        ]
        sums[low] += low_side[0] * projected[0] + low_side[1] * projected[1]
        sums[high] += high_side[0] * projected[0] + high_side[1] * projected[1]
        return carry

    lax.fori_loop(0, blocks, add_block, 0, unroll=8)
    return [jnp.sum(sums[at], axis=0, keepdims=True) for at in range(clusters)]


def total_of(value):
    return jnp.sum(jnp.sum(value, axis=1, keepdims=True), axis=0, keepdims=True)


def begin_kernel(
    clusters_ref, factors_ref, vectors_ref, diag_ref, part_ref, state_ref, spread, sums
):
    damping = vectors_ref[0]
    residual = vectors_ref[1]
    precond = damping + diag_ref[...]
    direction = residual / precond
    state_ref[0] = damping
    state_ref[1] = precond
    state_ref[2] = jnp.zeros_like(residual)
    state_ref[3] = residual
    state_ref[4] = direction
    parts = system_part(clusters_ref, factors_ref, direction, spread, sums)
    for at, part in enumerate(parts):
        part_ref[at : at + 1] = part


def iterate_kernel(
    clusters_ref, factors_ref, state_ref, images_ref, part_ref, out_ref, spread, sums
):
    damping, precond, solution, residual, direction = [state_ref[at] for at in range(5)]
    images = gathered_sum(images_ref) + damping * direction
    fitness = total_of(residual * (residual / precond))
    step_size = fitness / total_of(direction * images)
    solution = solution + step_size * direction
    residual = residual - step_size * images
    scaled = residual / precond
    fitness_next = total_of(residual * scaled)
    direction = scaled + fitness_next / fitness * direction
    out_ref[0] = damping
    out_ref[1] = precond
    out_ref[2] = solution
    out_ref[3] = residual
    out_ref[4] = direction
    parts = system_part(clusters_ref, factors_ref, direction, spread, sums)
    curvature = sum(
        jnp.sum(direction[at : at + 1] * part, axis=1, keepdims=True)
        for at, part in enumerate(parts)
    )
    curvature = jnp.broadcast_to(curvature, parts[0].shape)
    tracks = part_ref.shape[0] // len(parts)
    for at, part in enumerate(parts):
        for track in range(tracks):
            part_ref[at * tracks + track, 0:1] = part
            part_ref[at * tracks + track, 1:2] = curvature


def finish_kernel(place_ref, state_ref, images_ref, solution_ref, scaled_ref, rows):
    damping, precond, _, residual, direction = [state_ref[at] for at in range(5)]
    for vector in range(5):
        for at in range(damping.shape[0]):
            rows[vector, at] = state_ref[vector, at : at + 1]
    row = place_ref[0]
    own = gathered_sum(images_ref)
    images = own[0:1] + rows[0, row] * rows[4, row]
    curvature = own[1:2, 0:1] + total_of(damping * direction * direction)
    step_size = total_of(residual * (residual / precond)) / curvature
    solution_ref[...] = rows[2, row] + step_size * rows[4, row]
    scaled_ref[...] = (rows[3, row] - step_size * images) / rows[1, row]


def on_device(factors, track_clusters, filed_flip, damping, rhs):
    n_row = lax.axis_size("row")
    n_col = lax.axis_size("col")
    n_track = lax.axis_size("track")
    params = factors.shape[3]
    clusters = n_row
    track_clusters = track_clusters.T
    spread = pltpu.VMEM((clusters, 8, params), jnp.float32)
    state_shape = jax.ShapeDtypeStruct((5, clusters, params), jnp.float32)

    def shape_of(*shape):
        return jax.ShapeDtypeStruct(shape, jnp.float32)

    squares = pl.pallas_call(
        diag_kernel,
        out_shape=shape_of(n_row, 2 * clusters, params),
        in_specs=[SMEM, VMEM, VMEM, VMEM],
        out_specs=VMEM,
        scratch_shapes=[spread],
        name="diag",
    )(track_clusters, factors, damping, rhs)
    early = pack(factors, track_clusters, filed_flip, EARLY, n_row, n_track)
    squares, vectors = pl.pallas_call(
        settle_kernel,
        out_shape=(shape_of(n_track, clusters, params), shape_of(2, clusters, params)),
        in_specs=[VMEM],
        out_specs=(VMEM, VMEM),
        name="settle",
    )(exchange(squares, "row"))
    squares = relay(exchange(squares, "track"), 1)[0]

    early, squares = lax.optimization_barrier((early, squares))
    early = exchange(early, ("row", "track"))
    part, state = pl.pallas_call(
        begin_kernel,
        out_shape=(shape_of(clusters, params), state_shape),
        in_specs=[SMEM] + [VMEM] * 3,
        out_specs=(VMEM, VMEM),
        scratch_shapes=[spread, spread],
        name="begin",
    )(track_clusters, factors, vectors, sum_over_planes(squares))
    part = sum_over_planes(part)
    part = jnp.broadcast_to(part[None], (n_row * n_track,) + part.shape)
    late = pack(factors, track_clusters, filed_flip, LATE, n_row, n_track)
    late, part, state = lax.optimization_barrier((late, part, state))
    late = exchange(late, ("row", "track"))
    track = lax.axis_index("track").astype(jnp.int32).reshape(1)
    blocks = early_products(track, early, params, n_col)
    late, part, blocks = lax.optimization_barrier((late, part, blocks))
    blocks = late_products(track, late, blocks, params).reshape(2 * params, params)
    piece = lax.psum_scatter(blocks, "col", scatter_dimension=0, tiled=True)

    part, state = pl.pallas_call(
        iterate_kernel,
        out_shape=(shape_of(n_row * n_track, 2, params), state_shape),
        in_specs=[SMEM] + [VMEM] * 3,
        out_specs=(VMEM, VMEM),
        scratch_shapes=[spread, spread],
        name="iterate",
    )(track_clusters, factors, state, exchange(part, ("row", "track")))
    part = exchange(relay(exchange(part, ("row", "track")), n_col), "col")
    piece, part = lax.optimization_barrier((piece, part))
    moves = [
        (
            plane_of(parity, track, part_at, n_col) * n_track + track,
            (2 * track + parity) * n_track + part_at,
        )
        for parity in range(2)
        for track in range(n_track)
        for part_at in range(n_track)
    ]
    blocks_out = lax.ppermute(piece, ("col", "track"), moves)[None, None]
    row_id = lax.axis_index("row").astype(jnp.int32).reshape(1)
    solution_out, scaled = pl.pallas_call(
        finish_kernel,
        out_shape=(shape_of(1, params), shape_of(1, params)),
        in_specs=[SMEM, VMEM, VMEM],
        out_specs=(VMEM, VMEM),
        scratch_shapes=[pltpu.VMEM((5, clusters, 1, params), jnp.float32)],
        name="finish",
    )(row_id, state, part)
    return solution_out, scaled, blocks_out


def solution(mesh):
    in_specs = (
        P(("row", "col", "track"), None, None, None),
        P(("row", "col", "track"), None),
        P(("row", "col", "track")),
        P("row", None),
        P("row", None),
    )
    out_specs = (P("row", None), P("row", None), P("row", "col", "track", None))
    return jax.shard_map(
        on_device, mesh=mesh, in_specs=in_specs, out_specs=out_specs, check_vma=False
    )
```

```python
import functools

import jax
import jax.numpy as jnp
from jax import lax
from jax.experimental import pallas as pl
from jax.experimental.pallas import tpu as pltpu
from jax.sharding import PartitionSpec as P

CAPACITY = 3
LANES = 128
PACK_STEPS = 8
GRAM_STEPS = 3


VMEM = pl.BlockSpec(memory_space=pltpu.VMEM)
SMEM = pl.BlockSpec(memory_space=pltpu.SMEM)


def tree_sum(parts):
    while len(parts) > 1:
        parts = [parts[at] + parts[at + 1] for at in range(0, len(parts), 2)]
    return parts[0]


def exchange(copies, axis):
    return lax.all_to_all(copies, axis, 0, 0, tiled=True)


def gathered_sum(ref):
    return tree_sum([ref[at] for at in range(ref.shape[0])])


def relay_kernel(in_ref, out_ref):
    out_ref[...] = jnp.broadcast_to(gathered_sum(in_ref)[None], out_ref.shape)


def relay(gathered, copies):
    shape = (copies,) + gathered.shape[1:]
    return pl.pallas_call(
        relay_kernel,
        out_shape=jax.ShapeDtypeStruct(shape, jnp.float32),
        in_specs=[VMEM],
        out_specs=VMEM,
        name="relay",
    )(gathered)


def sum_over_planes(value):
    planes = lax.axis_size("col")
    hop = 1
    while hop < planes:
        pairs = [(at, at ^ hop) for at in range(planes)]
        value = value + lax.ppermute(value, "col", pairs)
        hop *= 2
    return value


def pack_kernel(parity, tracks, clusters_ref, flip_ref, factors_ref, out_ref, counts, slots):
    step = pl.program_id(0)
    blocks, _, jac_rows, params = factors_ref.shape
    per_step = out_ref.shape[0]
    whole = params // LANES * LANES
    pairs = counts.shape[0]
    row_pairs = 2 * tracks

    @pl.when(step == 0)
    def _():
        def clear(pair, carry):
            counts[pair] = 0
            for place in range(CAPACITY):
                slots[pair * CAPACITY + place] = -1
            return carry

        lax.fori_loop(0, pairs, clear, 0, unroll=4)

        def assign(block, carry):
            flip = flip_ref[block]
            low = clusters_ref[0, block]
            high = clusters_ref[1, block]
            first = jnp.where(flip == 1, high, low)
            second = jnp.where(flip == 1, low, high)
            pair = first * row_pairs + second
            place = counts[pair]
            counts[pair] = place + 1
            slots[pair * CAPACITY + place] = block
            return carry

        lax.fori_loop(0, blocks, assign, 0, unroll=4)

    for local in range(per_step):
        for place in range(CAPACITY):
            pair = (step * per_step + local) * 2 + parity
            block = slots[pair * CAPACITY + place]

            @pl.when(block >= 0)
            def _():
                flip = flip_ref[block]
                first = factors_ref[block, flip]
                second = factors_ref[block, 1 - flip]
                out_ref[local, place, :, 0:whole] = first[:, 0:whole]
                out_ref[local, place, :, whole : whole + LANES] = jnp.concatenate(
                    [first[:, whole:params], second[:, whole:params]], axis=1
                )
                out_ref[local, place, :, whole + LANES : 2 * params] = second[:, 0:whole]

            @pl.when(block < 0)
            def _():
                out_ref[local, place] = jnp.zeros((jac_rows, 2 * params), jnp.float32)


def pack(factors, track_clusters, filed_flip, parity, rows, tracks):
    jac_rows, params = factors.shape[2:]
    shape = (rows * tracks, CAPACITY, jac_rows, 2 * params)
    pairs = 2 * rows * tracks
    return pl.pallas_call(
        functools.partial(pack_kernel, parity, tracks),
        grid=(PACK_STEPS,),
        out_shape=jax.ShapeDtypeStruct(shape, jnp.float32),
        in_specs=[
            SMEM,
            SMEM,
            pl.BlockSpec(factors.shape, lambda step: (0, 0, 0, 0)),
        ],
        out_specs=pl.BlockSpec(
            (shape[0] // PACK_STEPS,) + shape[1:], lambda step: (step, 0, 0, 0)
        ),
        scratch_shapes=[
            pltpu.SMEM((pairs,), jnp.int32),
            pltpu.SMEM((pairs * CAPACITY,), jnp.int32),
        ],
        cost_estimate=pl.CostEstimate(
            flops=0,
            bytes_accessed=4 * (factors.size + shape[0] * CAPACITY * jac_rows * 2 * params),
            transcendentals=0,
        ),
        name="pack",
    )(track_clusters, filed_flip, factors)


def gram_kernel(params, plane_ref, in_ref, *refs):
    out_refs, total = refs[:-1], refs[-1]
    step = pl.program_id(0)
    whole = params // LANES * LANES
    wide = whole + LANES
    value = in_ref[...]
    high = value.astype(jnp.bfloat16)
    low = (value - high.astype(jnp.float32)).astype(jnp.bfloat16)
    product = functools.partial(
        lax.dot_general,
        dimension_numbers=(((0,), (0,)), ((), ())),
        preferred_element_type=jnp.float32,
    )
    first, second = slice(0, wide), slice(whole, 2 * params)
    gram = product(high[:, first], high[:, second])
    gram = gram + product(high[:, first], low[:, second])
    gram = gram + product(low[:, first], high[:, second])

    @pl.when(step == 0)
    def _():
        total[...] = gram

    @pl.when(step > 0)
    def _():
        total[...] += gram

    @pl.when(step == pl.num_programs(0) - 1)
    def _():
        share = params // len(out_refs)
        for hop, out_ref in enumerate(out_refs):
            start = pl.multiple_of(jnp.bitwise_xor(plane_ref[0], hop) * share, 8)
            rows = pl.ds(start, share)
            out_ref[:, 0:whole] = total[rows, LANES:wide]
            out_ref[:, whole:params] = total[rows, params - whole : LANES]


def add_kernel(*refs):
    refs[-1][...] = tree_sum([ref[...] for ref in refs[:-1]])


def gram(plane, received, params, planes):
    received = received.reshape(-1, 2 * params)
    rows, width = received.shape
    wide = params // LANES * LANES + LANES
    share = params // planes
    return pl.pallas_call(
        functools.partial(gram_kernel, params),
        grid=(GRAM_STEPS,),
        out_shape=[jax.ShapeDtypeStruct((share, params), jnp.float32)] * planes,
        in_specs=[SMEM, pl.BlockSpec((rows // GRAM_STEPS, width), lambda step: (step, 0))],
        out_specs=[pl.BlockSpec((share, params), lambda step: (0, 0))] * planes,
        scratch_shapes=[pltpu.VMEM((wide, wide), jnp.float32)],
        cost_estimate=pl.CostEstimate(
            flops=6 * rows * wide * wide,
            bytes_accessed=4 * (rows * width + params * params),
            transcendentals=0,
        ),
        name="gram",
    )(plane, received)


def plane_rows(parts):
    planes = len(parts)
    came = [parts[0]]
    for hop in range(1, planes):
        pairs = [(at, at ^ hop) for at in range(planes)]
        came.append(lax.ppermute(parts[hop], "col", pairs))
    return pl.pallas_call(
        add_kernel,
        out_shape=jax.ShapeDtypeStruct(parts[0].shape, jnp.float32),
        in_specs=[VMEM] * planes,
        out_specs=VMEM,
        name="add",
    )(*came)


def placed(piece, parity):
    n_col = lax.axis_size("col")
    n_track = lax.axis_size("track")
    halves = n_col // n_track
    out = []
    for half in range(halves):
        moves = []
        for col in range(half, n_col, halves):
            for track in range(n_track):
                target = (2 * track + parity) * n_track + col // halves
                moves.append((col * n_track + track, target))
        out.append(lax.ppermute(piece, ("col", "track"), moves))
    return jnp.concatenate(out, axis=0)


def diag_kernel(clusters_ref, factors_ref, damping_ref, rhs_ref, out_ref, sums):
    blocks, sides, _, params = factors_ref.shape
    clusters = sums.shape[0]
    sums[...] = jnp.zeros_like(sums)

    def add_block(block, carry):
        for side in range(sides):
            value = factors_ref[block, side]
            squares = value * value
            sums[clusters_ref[side, block]] += squares[0:8] + squares[8:16]
        return carry

    lax.fori_loop(0, blocks, add_block, 0, unroll=4)
    for at in range(clusters):
        total = jnp.sum(sums[at], axis=0, keepdims=True)
        for copy in range(out_ref.shape[0]):
            out_ref[copy, at : at + 1] = total
    ids = lax.broadcasted_iota(jnp.int32, (clusters, params), 0)
    damping = jnp.broadcast_to(damping_ref[...], (clusters, params))
    rhs = jnp.broadcast_to(rhs_ref[...], (clusters, params))
    for copy in range(out_ref.shape[0]):
        out_ref[copy, clusters:] = jnp.where(ids == 0, damping, rhs)


def settle_kernel(in_ref, out_ref, vectors_ref):
    clusters = vectors_ref.shape[1]
    total = tree_sum([in_ref[at, 0:clusters] for at in range(in_ref.shape[0])])
    out_ref[...] = jnp.broadcast_to(total[None], out_ref.shape)
    for at in range(clusters):
        vectors_ref[0, at : at + 1] = in_ref[at, clusters : clusters + 1]
        vectors_ref[1, at : at + 1] = in_ref[at, clusters + 1 : clusters + 2]


def system_part(clusters_ref, factors_ref, direction, spread, sums):
    blocks = factors_ref.shape[0]
    clusters, params = direction.shape
    sums[...] = jnp.zeros_like(sums)
    for at in range(clusters):
        spread[at] = jnp.broadcast_to(direction[at : at + 1], (8, params))

    def add_block(block, carry):
        low = clusters_ref[0, block]
        high = clusters_ref[1, block]
        low_side = [factors_ref[block, 0, 0:8], factors_ref[block, 0, 8:16]]
        high_side = [factors_ref[block, 1, 0:8], factors_ref[block, 1, 8:16]]
        low_dir = spread[low]
        high_dir = spread[high]
        projected = [
            jnp.sum(one * low_dir + two * high_dir, axis=1, keepdims=True)
            for one, two in zip(low_side, high_side)
        ]
        sums[low] += low_side[0] * projected[0] + low_side[1] * projected[1]
        sums[high] += high_side[0] * projected[0] + high_side[1] * projected[1]
        return carry

    lax.fori_loop(0, blocks, add_block, 0, unroll=8)
    return [jnp.sum(sums[at], axis=0, keepdims=True) for at in range(clusters)]


def total_of(value):
    return jnp.sum(jnp.sum(value, axis=1, keepdims=True), axis=0, keepdims=True)


def begin_kernel(
    clusters_ref, factors_ref, vectors_ref, diag_ref, part_ref, state_ref, spread, sums
):
    damping = vectors_ref[0]
    residual = vectors_ref[1]
    precond = damping + diag_ref[...]
    direction = residual / precond
    state_ref[0] = damping
    state_ref[1] = precond
    state_ref[2] = jnp.zeros_like(residual)
    state_ref[3] = residual
    state_ref[4] = direction
    parts = system_part(clusters_ref, factors_ref, direction, spread, sums)
    for at, part in enumerate(parts):
        part_ref[at : at + 1] = part


def iterate_kernel(
    clusters_ref, factors_ref, state_ref, images_ref, part_ref, out_ref, spread, sums
):
    damping, precond, solution, residual, direction = [state_ref[at] for at in range(5)]
    images = gathered_sum(images_ref) + damping * direction
    fitness = total_of(residual * (residual / precond))
    step_size = fitness / total_of(direction * images)
    solution = solution + step_size * direction
    residual = residual - step_size * images
    scaled = residual / precond
    fitness_next = total_of(residual * scaled)
    direction = scaled + fitness_next / fitness * direction
    out_ref[0] = damping
    out_ref[1] = precond
    out_ref[2] = solution
    out_ref[3] = residual
    out_ref[4] = direction
    parts = system_part(clusters_ref, factors_ref, direction, spread, sums)
    curvature = sum(
        jnp.sum(direction[at : at + 1] * part, axis=1, keepdims=True)
        for at, part in enumerate(parts)
    )
    curvature = jnp.broadcast_to(curvature, parts[0].shape)
    tracks = part_ref.shape[0] // len(parts)
    for at, part in enumerate(parts):
        for track in range(tracks):
            part_ref[at * tracks + track, 0:1] = part
            part_ref[at * tracks + track, 1:2] = curvature


def finish_kernel(place_ref, state_ref, images_ref, solution_ref, scaled_ref, rows):
    damping, precond, _, residual, direction = [state_ref[at] for at in range(5)]
    for vector in range(5):
        for at in range(damping.shape[0]):
            rows[vector, at] = state_ref[vector, at : at + 1]
    row = place_ref[0]
    own = gathered_sum(images_ref)
    images = own[0:1] + rows[0, row] * rows[4, row]
    curvature = own[1:2, 0:1] + total_of(damping * direction * direction)
    step_size = total_of(residual * (residual / precond)) / curvature
    solution_ref[...] = rows[2, row] + step_size * rows[4, row]
    scaled_ref[...] = (rows[3, row] - step_size * images) / rows[1, row]


def on_device(factors, track_clusters, filed_flip, damping, rhs):
    n_row = lax.axis_size("row")
    n_col = lax.axis_size("col")
    n_track = lax.axis_size("track")
    params = factors.shape[3]
    clusters = n_row
    track_clusters = track_clusters.T
    spread = pltpu.VMEM((clusters, 8, params), jnp.float32)
    state_shape = jax.ShapeDtypeStruct((5, clusters, params), jnp.float32)

    def shape_of(*shape):
        return jax.ShapeDtypeStruct(shape, jnp.float32)

    squares = pl.pallas_call(
        diag_kernel,
        out_shape=shape_of(n_row, 2 * clusters, params),
        in_specs=[SMEM, VMEM, VMEM, VMEM],
        out_specs=VMEM,
        scratch_shapes=[spread],
        name="diag",
    )(track_clusters, factors, damping, rhs)
    even = pack(factors, track_clusters, filed_flip, 0, n_row, n_track)
    squares, vectors = pl.pallas_call(
        settle_kernel,
        out_shape=(shape_of(n_track, clusters, params), shape_of(2, clusters, params)),
        in_specs=[VMEM],
        out_specs=(VMEM, VMEM),
        name="settle",
    )(exchange(squares, "row"))
    squares = relay(exchange(squares, "track"), 1)[0]

    even, squares = lax.optimization_barrier((even, squares))
    even = exchange(even, ("row", "track"))
    part, state = pl.pallas_call(
        begin_kernel,
        out_shape=(shape_of(clusters, params), state_shape),
        in_specs=[SMEM] + [VMEM] * 3,
        out_specs=(VMEM, VMEM),
        scratch_shapes=[spread, spread],
        name="begin",
    )(track_clusters, factors, vectors, sum_over_planes(squares))
    part = sum_over_planes(part)
    part = jnp.broadcast_to(part[None], (n_row * n_track,) + part.shape)
    odd = pack(factors, track_clusters, filed_flip, 1, n_row, n_track)
    odd, part, state = lax.optimization_barrier((odd, part, state))
    odd = exchange(odd, ("row", "track"))
    plane = lax.axis_index("col").astype(jnp.int32).reshape(1)
    even = plane_rows(gram(plane, even, params, n_col))
    odd, part, even = lax.optimization_barrier((odd, part, even))
    odd = plane_rows(gram(plane, odd, params, n_col))

    part, state = pl.pallas_call(
        iterate_kernel,
        out_shape=(shape_of(n_row * n_track, 2, params), state_shape),
        in_specs=[SMEM] + [VMEM] * 3,
        out_specs=(VMEM, VMEM),
        scratch_shapes=[spread, spread],
        name="iterate",
    )(track_clusters, factors, state, exchange(part, ("row", "track")))
    part = relay(exchange(part, ("row", "track")), n_col)
    part, even, odd = lax.optimization_barrier((part, even, odd))
    even_out = placed(even, 0)
    odd_out = placed(odd, 1)
    part = exchange(part, "col")
    row_id = lax.axis_index("row").astype(jnp.int32).reshape(1)
    solution_out, scaled = pl.pallas_call(
        finish_kernel,
        out_shape=(shape_of(1, params), shape_of(1, params)),
        in_specs=[SMEM, VMEM, VMEM],
        out_specs=(VMEM, VMEM),
        scratch_shapes=[pltpu.VMEM((5, clusters, 1, params), jnp.float32)],
        name="finish",
    )(row_id, state, part)
    return solution_out, scaled, (even_out + odd_out)[None, None]


def solution(mesh):
    in_specs = (
        P(("row", "col", "track"), None, None, None),
        P(("row", "col", "track"), None),
        P(("row", "col", "track")),
        P("row", None),
        P("row", None),
    )
    out_specs = (P("row", None), P("row", None), P("row", "col", "track", None))
    return jax.shard_map(
        on_device, mesh=mesh, in_specs=in_specs, out_specs=out_specs, check_vma=False
    )
```

```python
import functools

import jax
import jax.numpy as jnp
from jax import lax
from jax.experimental import pallas as pl
from jax.experimental.pallas import tpu as pltpu
from jax.sharding import PartitionSpec as P

CAPACITY = 3
LANES = 128
PACK_STEPS = 8
GRAM_STEPS = 3


VMEM = pl.BlockSpec(memory_space=pltpu.VMEM)
SMEM = pl.BlockSpec(memory_space=pltpu.SMEM)


def tree_sum(parts):
    while len(parts) > 1:
        parts = [parts[at] + parts[at + 1] for at in range(0, len(parts), 2)]
    return parts[0]


def exchange(copies, axis):
    return lax.all_to_all(copies, axis, 0, 0, tiled=True)


def gathered_sum(ref):
    return tree_sum([ref[at] for at in range(ref.shape[0])])


def relay_kernel(in_ref, out_ref):
    out_ref[...] = jnp.broadcast_to(gathered_sum(in_ref)[None], out_ref.shape)


def relay(gathered, copies):
    shape = (copies,) + gathered.shape[1:]
    return pl.pallas_call(
        relay_kernel,
        out_shape=jax.ShapeDtypeStruct(shape, jnp.float32),
        in_specs=[VMEM],
        out_specs=VMEM,
        name="relay",
    )(gathered)


def sum_over_planes(value):
    planes = lax.axis_size("col")
    hop = 1
    while hop < planes:
        pairs = [(at, at ^ hop) for at in range(planes)]
        value = value + lax.ppermute(value, "col", pairs)
        hop *= 2
    return value


def pack_kernel(parity, tracks, clusters_ref, flip_ref, factors_ref, out_ref, counts, slots):
    step = pl.program_id(0)
    blocks, _, jac_rows, params = factors_ref.shape
    per_step = out_ref.shape[0]
    whole = params // LANES * LANES
    pairs = counts.shape[0]
    row_pairs = 2 * tracks

    @pl.when(step == 0)
    def _():
        def clear(pair, carry):
            counts[pair] = 0
            for place in range(CAPACITY):
                slots[pair * CAPACITY + place] = -1
            return carry

        lax.fori_loop(0, pairs, clear, 0, unroll=4)

        def assign(block, carry):
            flip = flip_ref[block]
            low = clusters_ref[0, block]
            high = clusters_ref[1, block]
            first = jnp.where(flip == 1, high, low)
            second = jnp.where(flip == 1, low, high)
            pair = first * row_pairs + second
            place = counts[pair]
            counts[pair] = place + 1
            slots[pair * CAPACITY + place] = block
            return carry

        lax.fori_loop(0, blocks, assign, 0, unroll=4)

    for local in range(per_step):
        for place in range(CAPACITY):
            pair = (step * per_step + local) * 2 + parity
            block = slots[pair * CAPACITY + place]

            @pl.when(block >= 0)
            def _():
                flip = flip_ref[block]
                first = factors_ref[block, flip]
                second = factors_ref[block, 1 - flip]
                out_ref[local, place, :, 0:whole] = first[:, 0:whole]
                out_ref[local, place, :, whole : whole + LANES] = jnp.concatenate(
                    [first[:, whole:params], second[:, whole:params]], axis=1
                )
                out_ref[local, place, :, whole + LANES : 2 * params] = second[:, 0:whole]

            @pl.when(block < 0)
            def _():
                out_ref[local, place] = jnp.zeros((jac_rows, 2 * params), jnp.float32)


def pack(factors, track_clusters, filed_flip, parity, rows, tracks):
    jac_rows, params = factors.shape[2:]
    shape = (rows * tracks, CAPACITY, jac_rows, 2 * params)
    pairs = 2 * rows * tracks
    return pl.pallas_call(
        functools.partial(pack_kernel, parity, tracks),
        grid=(PACK_STEPS,),
        out_shape=jax.ShapeDtypeStruct(shape, jnp.float32),
        in_specs=[
            SMEM,
            SMEM,
            pl.BlockSpec(factors.shape, lambda step: (0, 0, 0, 0)),
        ],
        out_specs=pl.BlockSpec(
            (shape[0] // PACK_STEPS,) + shape[1:], lambda step: (step, 0, 0, 0)
        ),
        scratch_shapes=[
            pltpu.SMEM((pairs,), jnp.int32),
            pltpu.SMEM((pairs * CAPACITY,), jnp.int32),
        ],
        cost_estimate=pl.CostEstimate(
            flops=0,
            bytes_accessed=4 * (factors.size + shape[0] * CAPACITY * jac_rows * 2 * params),
            transcendentals=0,
        ),
        name="pack",
    )(track_clusters, filed_flip, factors)


def gram_kernel(params, plane_ref, in_ref, *refs):
    out_refs, total = refs[:-1], refs[-1]
    step = pl.program_id(0)
    whole = params // LANES * LANES
    wide = whole + LANES
    value = in_ref[...]
    high = value.astype(jnp.bfloat16)
    low = (value - high.astype(jnp.float32)).astype(jnp.bfloat16)
    product = functools.partial(
        lax.dot_general,
        dimension_numbers=(((0,), (0,)), ((), ())),
        preferred_element_type=jnp.float32,
    )
    first, second = slice(0, wide), slice(whole, 2 * params)
    gram = product(high[:, first], high[:, second])
    gram = gram + product(high[:, first], low[:, second])
    gram = gram + product(low[:, first], high[:, second])

    @pl.when(step == 0)
    def _():
        total[...] = gram

    @pl.when(step > 0)
    def _():
        total[...] += gram

    @pl.when(step == pl.num_programs(0) - 1)
    def _():
        share = params // len(out_refs)
        for hop, out_ref in enumerate(out_refs):
            start = pl.multiple_of(jnp.bitwise_xor(plane_ref[0], hop) * share, 8)
            rows = pl.ds(start, share)
            out_ref[:, 0:whole] = total[rows, LANES:wide]
            out_ref[:, whole:params] = total[rows, params - whole : LANES]


def add_kernel(*refs):
    refs[-1][...] = tree_sum([ref[...] for ref in refs[:-1]])


def gram(plane, received, params, planes):
    received = received.reshape(-1, 2 * params)
    rows, width = received.shape
    wide = params // LANES * LANES + LANES
    share = params // planes
    return pl.pallas_call(
        functools.partial(gram_kernel, params),
        grid=(GRAM_STEPS,),
        out_shape=[jax.ShapeDtypeStruct((share, params), jnp.float32)] * planes,
        in_specs=[SMEM, pl.BlockSpec((rows // GRAM_STEPS, width), lambda step: (step, 0))],
        out_specs=[pl.BlockSpec((share, params), lambda step: (0, 0))] * planes,
        scratch_shapes=[pltpu.VMEM((wide, wide), jnp.float32)],
        cost_estimate=pl.CostEstimate(
            flops=6 * rows * wide * wide,
            bytes_accessed=4 * (rows * width + params * params),
            transcendentals=0,
        ),
        name="gram",
    )(plane, received)


def plane_rows(parts):
    planes = len(parts)
    came = [parts[0]]
    for hop in range(1, planes):
        pairs = [(at, at ^ hop) for at in range(planes)]
        came.append(lax.ppermute(parts[hop], "col", pairs))
    return pl.pallas_call(
        add_kernel,
        out_shape=jax.ShapeDtypeStruct(parts[0].shape, jnp.float32),
        in_specs=[VMEM] * planes,
        out_specs=VMEM,
        name="add",
    )(*came)


def placed(piece, parity):
    n_col = lax.axis_size("col")
    n_track = lax.axis_size("track")
    halves = n_col // n_track
    out = []
    for half in range(halves):
        moves = []
        for col in range(half, n_col, halves):
            for track in range(n_track):
                target = (2 * track + parity) * n_track + col // halves
                moves.append((col * n_track + track, target))
        out.append(lax.ppermute(piece, ("col", "track"), moves))
    return jnp.concatenate(out, axis=0)


def diag_kernel(clusters_ref, factors_ref, damping_ref, rhs_ref, out_ref, sums):
    blocks, sides, _, params = factors_ref.shape
    clusters = sums.shape[0]
    sums[...] = jnp.zeros_like(sums)

    def add_block(block, carry):
        for side in range(sides):
            value = factors_ref[block, side]
            squares = value * value
            sums[clusters_ref[side, block]] += squares[0:8] + squares[8:16]
        return carry

    lax.fori_loop(0, blocks, add_block, 0, unroll=4)
    for at in range(clusters):
        total = jnp.sum(sums[at], axis=0, keepdims=True)
        for copy in range(out_ref.shape[0]):
            out_ref[copy, at : at + 1] = total
    ids = lax.broadcasted_iota(jnp.int32, (clusters, params), 0)
    damping = jnp.broadcast_to(damping_ref[...], (clusters, params))
    rhs = jnp.broadcast_to(rhs_ref[...], (clusters, params))
    for copy in range(out_ref.shape[0]):
        out_ref[copy, clusters:] = jnp.where(ids == 0, damping, rhs)


def settle_kernel(in_ref, out_ref, vectors_ref):
    clusters = vectors_ref.shape[1]
    total = tree_sum([in_ref[at, 0:clusters] for at in range(in_ref.shape[0])])
    out_ref[...] = jnp.broadcast_to(total[None], out_ref.shape)
    for at in range(clusters):
        vectors_ref[0, at : at + 1] = in_ref[at, clusters : clusters + 1]
        vectors_ref[1, at : at + 1] = in_ref[at, clusters + 1 : clusters + 2]


def system_part(clusters_ref, factors_ref, direction, spread, sums):
    blocks = factors_ref.shape[0]
    clusters, params = direction.shape
    sums[...] = jnp.zeros_like(sums)
    for at in range(clusters):
        spread[at] = jnp.broadcast_to(direction[at : at + 1], (8, params))

    def add_block(block, carry):
        low = clusters_ref[0, block]
        high = clusters_ref[1, block]
        low_side = [factors_ref[block, 0, 0:8], factors_ref[block, 0, 8:16]]
        high_side = [factors_ref[block, 1, 0:8], factors_ref[block, 1, 8:16]]
        low_dir = spread[low]
        high_dir = spread[high]
        projected = [
            jnp.sum(one * low_dir + two * high_dir, axis=1, keepdims=True)
            for one, two in zip(low_side, high_side)
        ]
        sums[low] += low_side[0] * projected[0] + low_side[1] * projected[1]
        sums[high] += high_side[0] * projected[0] + high_side[1] * projected[1]
        return carry

    lax.fori_loop(0, blocks, add_block, 0, unroll=8)
    return [jnp.sum(sums[at], axis=0, keepdims=True) for at in range(clusters)]


def total_of(value):
    return jnp.sum(jnp.sum(value, axis=1, keepdims=True), axis=0, keepdims=True)


def begin_kernel(
    clusters_ref, factors_ref, vectors_ref, diag_ref, part_ref, state_ref, spread, sums
):
    damping = vectors_ref[0]
    residual = vectors_ref[1]
    precond = damping + diag_ref[...]
    direction = residual / precond
    state_ref[0] = damping
    state_ref[1] = precond
    state_ref[2] = jnp.zeros_like(residual)
    state_ref[3] = residual
    state_ref[4] = direction
    parts = system_part(clusters_ref, factors_ref, direction, spread, sums)
    for at, part in enumerate(parts):
        part_ref[at : at + 1] = part


def iterate_kernel(
    clusters_ref, factors_ref, state_ref, images_ref, part_ref, out_ref, spread, sums
):
    damping, precond, solution, residual, direction = [state_ref[at] for at in range(5)]
    images = gathered_sum(images_ref) + damping * direction
    fitness = total_of(residual * (residual / precond))
    step_size = fitness / total_of(direction * images)
    solution = solution + step_size * direction
    residual = residual - step_size * images
    scaled = residual / precond
    fitness_next = total_of(residual * scaled)
    direction = scaled + fitness_next / fitness * direction
    out_ref[0] = damping
    out_ref[1] = precond
    out_ref[2] = solution
    out_ref[3] = residual
    out_ref[4] = direction
    parts = system_part(clusters_ref, factors_ref, direction, spread, sums)
    curvature = sum(
        jnp.sum(direction[at : at + 1] * part, axis=1, keepdims=True)
        for at, part in enumerate(parts)
    )
    curvature = jnp.broadcast_to(curvature, parts[0].shape)
    tracks = part_ref.shape[0] // len(parts)
    for at, part in enumerate(parts):
        for track in range(tracks):
            part_ref[at * tracks + track, 0:1] = part
            part_ref[at * tracks + track, 1:2] = curvature


def finish_kernel(place_ref, state_ref, images_ref, solution_ref, scaled_ref, rows):
    damping, precond, _, residual, direction = [state_ref[at] for at in range(5)]
    for vector in range(5):
        for at in range(damping.shape[0]):
            rows[vector, at] = state_ref[vector, at : at + 1]
    row = place_ref[0]
    own = gathered_sum(images_ref)
    images = own[0:1] + rows[0, row] * rows[4, row]
    curvature = own[1:2, 0:1] + total_of(damping * direction * direction)
    step_size = total_of(residual * (residual / precond)) / curvature
    solution_ref[...] = rows[2, row] + step_size * rows[4, row]
    scaled_ref[...] = (rows[3, row] - step_size * images) / rows[1, row]


def on_device(factors, track_clusters, filed_flip, damping, rhs):
    n_row = lax.axis_size("row")
    n_col = lax.axis_size("col")
    n_track = lax.axis_size("track")
    params = factors.shape[3]
    clusters = n_row
    track_clusters = track_clusters.T
    spread = pltpu.VMEM((clusters, 8, params), jnp.float32)
    state_shape = jax.ShapeDtypeStruct((5, clusters, params), jnp.float32)

    def shape_of(*shape):
        return jax.ShapeDtypeStruct(shape, jnp.float32)

    squares = pl.pallas_call(
        diag_kernel,
        out_shape=shape_of(n_row, 2 * clusters, params),
        in_specs=[SMEM, VMEM, VMEM, VMEM],
        out_specs=VMEM,
        scratch_shapes=[spread],
        name="diag",
    )(track_clusters, factors, damping, rhs)
    even = pack(factors, track_clusters, filed_flip, 0, n_row, n_track)
    squares, vectors = pl.pallas_call(
        settle_kernel,
        out_shape=(shape_of(n_track, clusters, params), shape_of(2, clusters, params)),
        in_specs=[VMEM],
        out_specs=(VMEM, VMEM),
        name="settle",
    )(exchange(squares, "row"))
    squares = relay(exchange(squares, "track"), 1)[0]

    even, squares = lax.optimization_barrier((even, squares))
    even = exchange(even, ("row", "track"))
    part, state = pl.pallas_call(
        begin_kernel,
        out_shape=(shape_of(clusters, params), state_shape),
        in_specs=[SMEM] + [VMEM] * 3,
        out_specs=(VMEM, VMEM),
        scratch_shapes=[spread, spread],
        name="begin",
    )(track_clusters, factors, vectors, sum_over_planes(squares))
    part = sum_over_planes(part)
    part = jnp.broadcast_to(part[None], (n_row * n_track,) + part.shape)
    odd = pack(factors, track_clusters, filed_flip, 1, n_row, n_track)
    odd, part, state = lax.optimization_barrier((odd, part, state))
    odd = exchange(odd, ("row", "track"))
    plane = lax.axis_index("col").astype(jnp.int32).reshape(1)
    even = plane_rows(gram(plane, even, params, n_col))
    odd, part, even = lax.optimization_barrier((odd, part, even))
    even = placed(even, 0)
    odd = plane_rows(gram(plane, odd, params, n_col))

    part, state = pl.pallas_call(
        iterate_kernel,
        out_shape=(shape_of(n_row * n_track, 2, params), state_shape),
        in_specs=[SMEM] + [VMEM] * 3,
        out_specs=(VMEM, VMEM),
        scratch_shapes=[spread, spread],
        name="iterate",
    )(track_clusters, factors, state, exchange(part, ("row", "track")))
    part, even = lax.optimization_barrier((part, even))
    part = relay(exchange(part, ("row", "track")), n_col)
    part, odd = lax.optimization_barrier((part, odd))
    odd = placed(odd, 1)
    part = exchange(part, "col")
    row_id = lax.axis_index("row").astype(jnp.int32).reshape(1)
    solution_out, scaled = pl.pallas_call(
        finish_kernel,
        out_shape=(shape_of(1, params), shape_of(1, params)),
        in_specs=[SMEM, VMEM, VMEM],
        out_specs=(VMEM, VMEM),
        scratch_shapes=[pltpu.VMEM((5, clusters, 1, params), jnp.float32)],
        name="finish",
    )(row_id, state, part)
    return solution_out, scaled, (even + odd)[None, None]


def solution(mesh):
    in_specs = (
        P(("row", "col", "track"), None, None, None),
        P(("row", "col", "track"), None),
        P(("row", "col", "track")),
        P("row", None),
        P("row", None),
    )
    out_specs = (P("row", None), P("row", None), P("row", "col", "track", None))
    return jax.shard_map(
        on_device, mesh=mesh, in_specs=in_specs, out_specs=out_specs, check_vma=False
    )
```

```python
import functools

import jax
import jax.numpy as jnp
from jax import lax
from jax.experimental import pallas as pl
from jax.experimental.pallas import tpu as pltpu
from jax.sharding import PartitionSpec as P

CAPACITY = 3
LANES = 128
PACK_STEPS = 8
GRAM_STEPS = 3


VMEM = pl.BlockSpec(memory_space=pltpu.VMEM)
SMEM = pl.BlockSpec(memory_space=pltpu.SMEM)


def tree_sum(parts):
    while len(parts) > 1:
        parts = [parts[at] + parts[at + 1] for at in range(0, len(parts), 2)]
    return parts[0]


def exchange(copies, axis):
    return lax.all_to_all(copies, axis, 0, 0, tiled=True)


def gathered_sum(ref):
    return tree_sum([ref[at] for at in range(ref.shape[0])])


def relay_kernel(in_ref, out_ref):
    out_ref[...] = jnp.broadcast_to(gathered_sum(in_ref)[None], out_ref.shape)


def relay(gathered, copies):
    shape = (copies,) + gathered.shape[1:]
    return pl.pallas_call(
        relay_kernel,
        out_shape=jax.ShapeDtypeStruct(shape, jnp.float32),
        in_specs=[VMEM],
        out_specs=VMEM,
        name="relay",
    )(gathered)


def sum_over_planes(value):
    planes = lax.axis_size("col")
    hop = 1
    while hop < planes:
        pairs = [(at, at ^ hop) for at in range(planes)]
        value = value + lax.ppermute(value, "col", pairs)
        hop *= 2
    return value


def pack_kernel(parity, tracks, clusters_ref, flip_ref, factors_ref, out_ref, counts, slots):
    step = pl.program_id(0)
    blocks, _, jac_rows, params = factors_ref.shape
    per_step = out_ref.shape[0]
    whole = params // LANES * LANES
    pairs = counts.shape[0]
    row_pairs = 2 * tracks

    @pl.when(step == 0)
    def _():
        def clear(pair, carry):
            counts[pair] = 0
            for place in range(CAPACITY):
                slots[pair * CAPACITY + place] = -1
            return carry

        lax.fori_loop(0, pairs, clear, 0, unroll=4)

        def assign(block, carry):
            flip = flip_ref[block]
            low = clusters_ref[0, block]
            high = clusters_ref[1, block]
            first = jnp.where(flip == 1, high, low)
            second = jnp.where(flip == 1, low, high)
            pair = first * row_pairs + second
            place = counts[pair]
            counts[pair] = place + 1
            slots[pair * CAPACITY + place] = block
            return carry

        lax.fori_loop(0, blocks, assign, 0, unroll=4)

    for local in range(per_step):
        for place in range(CAPACITY):
            pair = (step * per_step + local) * 2 + parity
            block = slots[pair * CAPACITY + place]

            @pl.when(block >= 0)
            def _():
                flip = flip_ref[block]
                first = factors_ref[block, flip]
                second = factors_ref[block, 1 - flip]
                out_ref[local, place, :, 0:whole] = first[:, 0:whole]
                out_ref[local, place, :, whole : whole + LANES] = jnp.concatenate(
                    [first[:, whole:params], second[:, whole:params]], axis=1
                )
                out_ref[local, place, :, whole + LANES : 2 * params] = second[:, 0:whole]

            @pl.when(block < 0)
            def _():
                out_ref[local, place] = jnp.zeros((jac_rows, 2 * params), jnp.float32)


def pack(factors, track_clusters, filed_flip, parity, rows, tracks):
    jac_rows, params = factors.shape[2:]
    shape = (rows * tracks, CAPACITY, jac_rows, 2 * params)
    pairs = 2 * rows * tracks
    return pl.pallas_call(
        functools.partial(pack_kernel, parity, tracks),
        grid=(PACK_STEPS,),
        out_shape=jax.ShapeDtypeStruct(shape, jnp.float32),
        in_specs=[
            SMEM,
            SMEM,
            pl.BlockSpec(factors.shape, lambda step: (0, 0, 0, 0)),
        ],
        out_specs=pl.BlockSpec(
            (shape[0] // PACK_STEPS,) + shape[1:], lambda step: (step, 0, 0, 0)
        ),
        scratch_shapes=[
            pltpu.SMEM((pairs,), jnp.int32),
            pltpu.SMEM((pairs * CAPACITY,), jnp.int32),
        ],
        cost_estimate=pl.CostEstimate(
            flops=0,
            bytes_accessed=4 * (factors.size + shape[0] * CAPACITY * jac_rows * 2 * params),
            transcendentals=0,
        ),
        name="pack",
    )(track_clusters, filed_flip, factors)


def gram_kernel(params, plane_ref, in_ref, *refs):
    out_refs, total = refs[:-1], refs[-1]
    step = pl.program_id(0)
    whole = params // LANES * LANES
    wide = whole + LANES
    value = in_ref[...]
    high = value.astype(jnp.bfloat16)
    low = (value - high.astype(jnp.float32)).astype(jnp.bfloat16)
    product = functools.partial(
        lax.dot_general,
        dimension_numbers=(((0,), (0,)), ((), ())),
        preferred_element_type=jnp.float32,
    )
    first, second = slice(0, wide), slice(whole, 2 * params)
    gram = product(high[:, first], high[:, second])
    gram = gram + product(high[:, first], low[:, second])
    gram = gram + product(low[:, first], high[:, second])

    @pl.when(step == 0)
    def _():
        total[...] = gram

    @pl.when(step > 0)
    def _():
        total[...] += gram

    @pl.when(step == pl.num_programs(0) - 1)
    def _():
        share = params // len(out_refs)
        for hop, out_ref in enumerate(out_refs):
            start = pl.multiple_of(jnp.bitwise_xor(plane_ref[0], hop) * share, 8)
            rows = pl.ds(start, share)
            out_ref[:, 0:whole] = total[rows, LANES:wide]
            out_ref[:, whole:params] = total[rows, params - whole : LANES]


def add_kernel(*refs):
    refs[-1][...] = tree_sum([ref[...] for ref in refs[:-1]])


def gram(plane, received, params, planes):
    received = received.reshape(-1, 2 * params)
    rows, width = received.shape
    wide = params // LANES * LANES + LANES
    share = params // planes
    return pl.pallas_call(
        functools.partial(gram_kernel, params),
        grid=(GRAM_STEPS,),
        out_shape=[jax.ShapeDtypeStruct((share, params), jnp.float32)] * planes,
        in_specs=[SMEM, pl.BlockSpec((rows // GRAM_STEPS, width), lambda step: (step, 0))],
        out_specs=[pl.BlockSpec((share, params), lambda step: (0, 0))] * planes,
        scratch_shapes=[pltpu.VMEM((wide, wide), jnp.float32)],
        cost_estimate=pl.CostEstimate(
            flops=6 * rows * wide * wide,
            bytes_accessed=4 * (rows * width + params * params),
            transcendentals=0,
        ),
        name="gram",
    )(plane, received)


def plane_rows(parts):
    planes = len(parts)
    came = [parts[0]]
    for hop in range(1, planes):
        pairs = [(at, at ^ hop) for at in range(planes)]
        came.append(lax.ppermute(parts[hop], "col", pairs))
    return pl.pallas_call(
        add_kernel,
        out_shape=jax.ShapeDtypeStruct(parts[0].shape, jnp.float32),
        in_specs=[VMEM] * planes,
        out_specs=VMEM,
        name="add",
    )(*came)


def placed(piece, parity):
    n_col = lax.axis_size("col")
    n_track = lax.axis_size("track")
    halves = n_col // n_track
    out = []
    for half in range(halves):
        moves = []
        for col in range(half, n_col, halves):
            for track in range(n_track):
                target = (2 * track + parity) * n_track + col // halves
                moves.append((col * n_track + track, target))
        out.append(lax.ppermute(piece, ("col", "track"), moves))
    return jnp.concatenate(out, axis=0)


def diag_kernel(clusters_ref, factors_ref, damping_ref, rhs_ref, out_ref, sums):
    blocks, sides, _, params = factors_ref.shape
    clusters = sums.shape[0]
    sums[...] = jnp.zeros_like(sums)

    def add_block(block, carry):
        for side in range(sides):
            value = factors_ref[block, side]
            squares = value * value
            sums[clusters_ref[side, block]] += squares[0:8] + squares[8:16]
        return carry

    lax.fori_loop(0, blocks, add_block, 0, unroll=4)
    for at in range(clusters):
        total = jnp.sum(sums[at], axis=0, keepdims=True)
        for copy in range(out_ref.shape[0]):
            out_ref[copy, at : at + 1] = total
    ids = lax.broadcasted_iota(jnp.int32, (clusters, params), 0)
    damping = jnp.broadcast_to(damping_ref[...], (clusters, params))
    rhs = jnp.broadcast_to(rhs_ref[...], (clusters, params))
    for copy in range(out_ref.shape[0]):
        out_ref[copy, clusters:] = jnp.where(ids == 0, damping, rhs)


def settle_kernel(in_ref, out_ref, vectors_ref):
    clusters = vectors_ref.shape[1]
    total = tree_sum([in_ref[at, 0:clusters] for at in range(in_ref.shape[0])])
    out_ref[...] = jnp.broadcast_to(total[None], out_ref.shape)
    for at in range(clusters):
        vectors_ref[0, at : at + 1] = in_ref[at, clusters : clusters + 1]
        vectors_ref[1, at : at + 1] = in_ref[at, clusters + 1 : clusters + 2]


def system_part(clusters_ref, factors_ref, direction, spread, sums):
    blocks = factors_ref.shape[0]
    clusters, params = direction.shape
    sums[...] = jnp.zeros_like(sums)
    for at in range(clusters):
        spread[at] = jnp.broadcast_to(direction[at : at + 1], (8, params))

    def add_block(block, carry):
        low = clusters_ref[0, block]
        high = clusters_ref[1, block]
        low_side = [factors_ref[block, 0, 0:8], factors_ref[block, 0, 8:16]]
        high_side = [factors_ref[block, 1, 0:8], factors_ref[block, 1, 8:16]]
        low_dir = spread[low]
        high_dir = spread[high]
        projected = [
            jnp.sum(one * low_dir + two * high_dir, axis=1, keepdims=True)
            for one, two in zip(low_side, high_side)
        ]
        sums[low] += low_side[0] * projected[0] + low_side[1] * projected[1]
        sums[high] += high_side[0] * projected[0] + high_side[1] * projected[1]
        return carry

    lax.fori_loop(0, blocks, add_block, 0, unroll=8)
    return [jnp.sum(sums[at], axis=0, keepdims=True) for at in range(clusters)]


def total_of(value):
    return jnp.sum(jnp.sum(value, axis=1, keepdims=True), axis=0, keepdims=True)


def begin_kernel(
    clusters_ref, factors_ref, vectors_ref, diag_ref, part_ref, state_ref, spread, sums
):
    damping = vectors_ref[0]
    residual = vectors_ref[1]
    precond = damping + diag_ref[...]
    direction = residual / precond
    state_ref[0] = damping
    state_ref[1] = precond
    state_ref[2] = jnp.zeros_like(residual)
    state_ref[3] = residual
    state_ref[4] = direction
    parts = system_part(clusters_ref, factors_ref, direction, spread, sums)
    for at, part in enumerate(parts):
        part_ref[at : at + 1] = part


def iterate_kernel(
    clusters_ref, factors_ref, state_ref, images_ref, part_ref, out_ref, spread, sums
):
    damping, precond, solution, residual, direction = [state_ref[at] for at in range(5)]
    images = gathered_sum(images_ref) + damping * direction
    fitness = total_of(residual * (residual / precond))
    step_size = fitness / total_of(direction * images)
    solution = solution + step_size * direction
    residual = residual - step_size * images
    scaled = residual / precond
    fitness_next = total_of(residual * scaled)
    direction = scaled + fitness_next / fitness * direction
    out_ref[0] = damping
    out_ref[1] = precond
    out_ref[2] = solution
    out_ref[3] = residual
    out_ref[4] = direction
    parts = system_part(clusters_ref, factors_ref, direction, spread, sums)
    curvature = sum(
        jnp.sum(direction[at : at + 1] * part, axis=1, keepdims=True)
        for at, part in enumerate(parts)
    )
    curvature = jnp.broadcast_to(curvature, parts[0].shape)
    tracks = part_ref.shape[0] // len(parts)
    for at, part in enumerate(parts):
        for track in range(tracks):
            part_ref[at * tracks + track, 0:1] = part
            part_ref[at * tracks + track, 1:2] = curvature


def finish_kernel(place_ref, state_ref, images_ref, solution_ref, scaled_ref, rows):
    damping, precond, _, residual, direction = [state_ref[at] for at in range(5)]
    for vector in range(5):
        for at in range(damping.shape[0]):
            rows[vector, at] = state_ref[vector, at : at + 1]
    row = place_ref[0]
    own = gathered_sum(images_ref)
    images = own[0:1] + rows[0, row] * rows[4, row]
    curvature = own[1:2, 0:1] + total_of(damping * direction * direction)
    step_size = total_of(residual * (residual / precond)) / curvature
    solution_ref[...] = rows[2, row] + step_size * rows[4, row]
    scaled_ref[...] = (rows[3, row] - step_size * images) / rows[1, row]


def on_device(factors, track_clusters, filed_flip, damping, rhs):
    n_row = lax.axis_size("row")
    n_col = lax.axis_size("col")
    n_track = lax.axis_size("track")
    params = factors.shape[3]
    clusters = n_row
    track_clusters = track_clusters.T
    spread = pltpu.VMEM((clusters, 8, params), jnp.float32)
    state_shape = jax.ShapeDtypeStruct((5, clusters, params), jnp.float32)

    def shape_of(*shape):
        return jax.ShapeDtypeStruct(shape, jnp.float32)

    squares = pl.pallas_call(
        diag_kernel,
        out_shape=shape_of(n_row, 2 * clusters, params),
        in_specs=[SMEM, VMEM, VMEM, VMEM],
        out_specs=VMEM,
        scratch_shapes=[spread],
        name="diag",
    )(track_clusters, factors, damping, rhs)
    even = pack(factors, track_clusters, filed_flip, 0, n_row, n_track)
    squares, vectors = pl.pallas_call(
        settle_kernel,
        out_shape=(shape_of(n_track, clusters, params), shape_of(2, clusters, params)),
        in_specs=[VMEM],
        out_specs=(VMEM, VMEM),
        name="settle",
    )(exchange(squares, "row"))
    squares = relay(exchange(squares, "track"), 1)[0]

    even, squares = lax.optimization_barrier((even, squares))
    even = exchange(even, ("row", "track"))
    part, state = pl.pallas_call(
        begin_kernel,
        out_shape=(shape_of(clusters, params), state_shape),
        in_specs=[SMEM] + [VMEM] * 3,
        out_specs=(VMEM, VMEM),
        scratch_shapes=[spread, spread],
        name="begin",
    )(track_clusters, factors, vectors, sum_over_planes(squares))
    part = sum_over_planes(part)
    part = jnp.broadcast_to(part[None], (n_row * n_track,) + part.shape)
    odd = pack(factors, track_clusters, filed_flip, 1, n_row, n_track)
    odd, part, state = lax.optimization_barrier((odd, part, state))
    odd = exchange(odd, ("row", "track"))
    plane = lax.axis_index("col").astype(jnp.int32).reshape(1)
    even = plane_rows(gram(plane, even, params, n_col))
    odd, part, even = lax.optimization_barrier((odd, part, even))
    even = placed(even, 0)
    odd = plane_rows(gram(plane, odd, params, n_col))

    part, state = pl.pallas_call(
        iterate_kernel,
        out_shape=(shape_of(n_row * n_track, 2, params), state_shape),
        in_specs=[SMEM] + [VMEM] * 3,
        out_specs=(VMEM, VMEM),
        scratch_shapes=[spread, spread],
        name="iterate",
    )(track_clusters, factors, state, exchange(part, ("row", "track")))
    part, even = lax.optimization_barrier((part, even))
    part = relay(exchange(part, ("row", "track")), n_col)
    part = exchange(part, "col")
    part, odd = lax.optimization_barrier((part, odd))
    odd = placed(odd, 1)
    row_id = lax.axis_index("row").astype(jnp.int32).reshape(1)
    solution_out, scaled = pl.pallas_call(
        finish_kernel,
        out_shape=(shape_of(1, params), shape_of(1, params)),
        in_specs=[SMEM, VMEM, VMEM],
        out_specs=(VMEM, VMEM),
        scratch_shapes=[pltpu.VMEM((5, clusters, 1, params), jnp.float32)],
        name="finish",
    )(row_id, state, part)
    return solution_out, scaled, (even + odd)[None, None]


def solution(mesh):
    in_specs = (
        P(("row", "col", "track"), None, None, None),
        P(("row", "col", "track"), None),
        P(("row", "col", "track")),
        P("row", None),
        P("row", None),
    )
    out_specs = (P("row", None), P("row", None), P("row", "col", "track", None))
    return jax.shard_map(
        on_device, mesh=mesh, in_specs=in_specs, out_specs=out_specs, check_vma=False
    )
```
